256 devices in a mesh: dap: 128 (over y, x_lo, z, core), ch: 2 (over x_hi).
Axes of the slice: x: 4 (x_hi: 2, x_lo: 2; x = x_hi * 2 + x_lo), y: 4, z: 8, core: 2. Of those that a mesh axis runs over, the one named last changes fastest.
Arguments:
- alignment_embedding: bfloat16 [128, 512, 256], P(None, 'dap'), may hold values from -6 to 6
- couple_embedding: bfloat16 [512, 512, 128], P('dap', 'ch'), may hold values from -6 to 6
- tensor_first_matrix: bfloat16 [256, 32], P(None, 'ch'), may hold values from -0.375 to 0.375
- tensor_second_matrix: bfloat16 [256, 32], replicated, may hold values from -0.375 to 0.375
- tensor_final_matrix: bfloat16 [1024, 128], P('ch'), may hold values from -1 to 1
- trimul_entry_matrix: bfloat16 [4, 128, 128], replicated, may hold values from -0.5 to 0.5
- trimul_sigmoid_matrix: bfloat16 [128, 128], replicated, may hold values from -0.5 to 0.5
- trimul_final_matrix: bfloat16 [128, 128], replicated, may hold values from -0.5 to 0.5
Outputs:
- pair_out: bfloat16 [512, 512, 128], P('dap', 'ch')
The draws below stay inside these ranges and needn't reach their ends.
All inputs are finite; a program needn't handle non-finite values.
Results may differ from the reference program's by a relative error of at most 0.014.
Values may be sent and summed in bfloat16 or wider, within the bound.
No kernel may reach another device: no remote copies, remote signals or barrier semaphores. Data moves between devices by JAX's collectives and lax.ppermute only.
A program may use at most 64 MiB of HBM per device.

```python
import jax
import jax.numpy as jnp
from jax import lax

ALIGNED_SEQS = 128
ALIGNMENT_FEAT = 256
CZ = 128
PROJ_WIDTH_SIDE = 32
CT = 128
ROWS_DEV = 4
AMINO_TOTAL = 512


def block_scale(rng, extent, pieces, low, high):
    factor_of, own = 1.0, jax.random.fold_in(rng, 6)
    for position, shards_of in pieces:
        steps = jnp.exp(jax.random.uniform(jax.random.fold_in(own, position), (shards_of,), jnp.float32, low / len(pieces), high / len(pieces)))
        factor_of = factor_of * jnp.repeat(steps, extent[position] // shards_of).reshape([-1 if axis == position else 1 for axis in range(len(extent))])
    return factor_of


def scatter_about(own_key, dims, spread, bound, pieces=(), dtype=jnp.bfloat16):
    level = block_scale(own_key, dims, pieces, -0.22, 0.18) if pieces else 1.0
    values = jax.random.normal(own_key, dims, jnp.float32) * spread * level
    return jnp.minimum(jnp.maximum(values, -bound), bound).astype(dtype)


def setup_inputs(seed: int = 0) -> dict:
    splits = jax.random.split(jax.random.key(seed), 9)
    alignment_embedding = scatter_about(splits[0], (ALIGNED_SEQS, AMINO_TOTAL, ALIGNMENT_FEAT), 1.0, 6.0, ((1, 128),))
    couple_embedding = scatter_about(splits[1], (AMINO_TOTAL, AMINO_TOTAL, CZ), 1.0, 6.0, ((0, 128), (1, 2)))
    tensor_first_matrix = scatter_about(splits[2], (ALIGNMENT_FEAT, PROJ_WIDTH_SIDE), ALIGNMENT_FEAT ** -0.5, 0.375, ((1, 2),))
    tensor_second_matrix = scatter_about(splits[3], (ALIGNMENT_FEAT, PROJ_WIDTH_SIDE), ALIGNMENT_FEAT ** -0.5, 0.375)
    tensor_final_matrix = scatter_about(splits[4], (PROJ_WIDTH_SIDE * PROJ_WIDTH_SIDE, CZ), PROJ_WIDTH_SIDE ** -0.5, 1.0, ((0, 2),))
    trimul_entry_matrix = scatter_about(splits[5], (4, CZ, CT), CZ ** -0.5, 0.5)
    trimul_sigmoid_matrix = scatter_about(splits[6], (CZ, CZ), CZ ** -0.5, 0.5)
    trimul_final_matrix = scatter_about(splits[7], (CT, CZ), CT ** -0.5, 0.5)
    return {"alignment_embedding": alignment_embedding, "couple_embedding": couple_embedding, "tensor_first_matrix": tensor_first_matrix, "tensor_second_matrix": tensor_second_matrix, "tensor_final_matrix": tensor_final_matrix, "trimul_entry_matrix": trimul_entry_matrix, "trimul_sigmoid_matrix": trimul_sigmoid_matrix, "trimul_final_matrix": trimul_final_matrix}


def standardize_fn(value, axis):
    mean = lax.optimization_barrier(jnp.mean(value, axis=axis, keepdims=True))
    centred = value - mean
    var = lax.optimization_barrier(jnp.mean(centred * centred, axis=axis, keepdims=True))
    return centred * lax.rsqrt(var + 1e-05)

def reference(alignment_embedding, couple_embedding, tensor_first_matrix, tensor_second_matrix, tensor_final_matrix, trimul_entry_matrix, trimul_sigmoid_matrix, trimul_final_matrix):
    alignment_standardized = standardize_fn(alignment_embedding.astype(jnp.float32), -1).astype(jnp.bfloat16)
    first_operand = jnp.einsum('ziv,vl->zil', alignment_standardized.astype(jnp.float32), tensor_first_matrix.astype(jnp.float32)).astype(jnp.bfloat16)
    second_operand = jnp.einsum('ziv,vl->zil', alignment_standardized.astype(jnp.float32), tensor_second_matrix.astype(jnp.float32)).astype(jnp.bfloat16)
    blocks = AMINO_TOTAL // ROWS_DEV
    left_blocks = jnp.transpose(first_operand.reshape(ALIGNED_SEQS, blocks, ROWS_DEV, PROJ_WIDTH_SIDE), (1, 0, 2, 3))
    right32 = second_operand.astype(jnp.float32)

    def block_update(left_block):
        outer = jnp.einsum('sic,sje->ijce', left_block.astype(jnp.float32), right32) * (1.0 / ALIGNED_SEQS)
        outer = outer.astype(jnp.bfloat16).reshape(ROWS_DEV * AMINO_TOTAL, PROJ_WIDTH_SIDE * PROJ_WIDTH_SIDE)
        return jnp.dot(outer, tensor_final_matrix, preferred_element_type=jnp.float32).reshape(ROWS_DEV, AMINO_TOTAL, CZ)
    update = lax.map(block_update, left_blocks).reshape(AMINO_TOTAL, AMINO_TOTAL, CZ)
    lifted = (couple_embedding.astype(jnp.float32) + update).astype(jnp.bfloat16)
    normed = standardize_fn(lifted.astype(jnp.float32), -1).astype(jnp.bfloat16)
    flat = normed.reshape(AMINO_TOTAL * AMINO_TOTAL, CZ)
    per_channel = jnp.transpose(trimul_entry_matrix, (2, 0, 1))

    def channel_product(weights):
        proj = jnp.dot(flat, jnp.transpose(weights), preferred_element_type=jnp.float32)
        left_t = (jax.nn.sigmoid(proj[:, 0]) * proj[:, 1]).astype(jnp.bfloat16).reshape(AMINO_TOTAL, AMINO_TOTAL)
        right_t = (jax.nn.sigmoid(proj[:, 2]) * proj[:, 3]).astype(jnp.bfloat16).reshape(AMINO_TOTAL, AMINO_TOTAL)
        return jnp.dot(left_t, jnp.transpose(right_t), preferred_element_type=jnp.float32).astype(jnp.bfloat16)
    tri = lax.map(channel_product, per_channel)
    tri_n = standardize_fn(tri.astype(jnp.float32), 0).astype(jnp.bfloat16)
    out = jnp.einsum('cij,cz->ijz', tri_n.astype(jnp.float32), trimul_final_matrix.astype(jnp.float32))
    gate = jax.nn.sigmoid(jnp.dot(flat, trimul_sigmoid_matrix, preferred_element_type=jnp.float32)).reshape(AMINO_TOTAL, AMINO_TOTAL, CZ)
    return (lifted.astype(jnp.float32) + gate * out).astype(jnp.bfloat16)
```

```python
import jax
import jax.numpy as jnp
from jax import lax
from jax.sharding import Mesh
from jax.sharding import PartitionSpec as P

DAP = ("yh", "yl", "xl", "z", "core")
PLANE = ("yl", "xl", "core")
CHIP = ("yh", "yl", "xl", "z", "xh")
F32 = jnp.float32
BF16 = jnp.bfloat16


def exchanged(x, axes):
    return lax.all_to_all(x, axes, split_axis=0, concat_axis=0, tiled=True)


def from_everyone(x, axes):
    copies = jnp.broadcast_to(x, (lax.axis_size(axes), *x.shape))
    return exchanged(copies, axes)


def partner(x, axis):
    return lax.ppermute(x, axis, [(0, 1), (1, 0)])


def standardize_fn(value, axis):
    mean = jnp.mean(value, axis=axis, keepdims=True)
    centred = value - mean
    var = jnp.mean(centred * centred, axis=axis, keepdims=True)
    return centred * lax.rsqrt(var + 1e-05)


def per_device(msa, couple, first, second, w_out, entry, w_gate, w_final):
    seqs = msa.shape[0]
    yh, xh, core = lax.axis_index("yh"), lax.axis_index("xh"), lax.axis_index("core")
    msa_n = standardize_fn(msa.astype(F32), -1).astype(BF16)
    right = jnp.einsum("siv,ve->eis", msa_n, second, preferred_element_type=F32).astype(BF16)
    right = jnp.where(yh == xh, right, partner(right, "yh"))
    right = from_everyone(right, "z")
    left = jnp.einsum("siv,vc->ics", msa_n, first, preferred_element_type=F32).astype(BF16)
    left = from_everyone(left.reshape(-1, seqs), PLANE + ("xh",))
    left = left.reshape(8, 2, 4, 16, seqs)
    w_other = partner(w_out, "xh")
    w_full = jnp.where(xh == 0, jnp.stack([w_out, w_other]), jnp.stack([w_other, w_out]))
    w_full = w_full.reshape(2, 16, 32, 128)

    block = couple.reshape(4, 2, 2, 8, 2, 4, 128).transpose(1, 2, 4, 0, 3, 5, 6)
    block = exchanged(block.reshape(8, 4, 32, 128), PLANE)
    outer = jnp.einsum("wejs,gxics->gijwexc", right, left, preferred_element_type=F32)
    outer = (outer * (1.0 / seqs)).astype(BF16)
    update = jnp.einsum("gijwexc,xcez->giwjz", outer, w_full, preferred_element_type=F32)
    lifted = (block.astype(F32) + update.reshape(8, 4, 32, 128)).astype(BF16)
    normed = standardize_fn(lifted.astype(F32), -1).astype(BF16)
    projected = jnp.einsum("gijz,qzc->qcgij", normed, entry, preferred_element_type=F32)
    left_t = (jax.nn.sigmoid(projected[0]) * projected[1]).astype(BF16).reshape(128, 8, 128)
    right_t = (jax.nn.sigmoid(projected[2]) * projected[3]).astype(BF16).reshape(128, 8, 128)
    cols = exchanged(jnp.concatenate([left_t, right_t], 1), CHIP)

    own = exchanged(lifted, PLANE)
    own = own.reshape(2, 2, 2, 4, 8, 4, 128).transpose(3, 0, 1, 4, 2, 5, 6).reshape(4, 256, 128)

    cols = cols.reshape(2, 2, 2, 8, 2, 2, 32, 32).transpose(5, 0, 3, 6, 1, 2, 4, 7)
    cols = cols.reshape(2, 512, 256)
    product = jnp.einsum("ik,jk->ij", cols[0], cols[1], preferred_element_type=F32)
    product = product.astype(BF16).reshape(2, 8, 2, 2, 2, 4, 512).transpose(4, 0, 2, 3, 1, 5, 6)
    product = product.reshape(2, 256, 512)
    mine = lax.dynamic_index_in_dim(product, core, 0, keepdims=False)
    theirs = partner(lax.dynamic_index_in_dim(product, 1 - core, 0, keepdims=False), "core")
    summed = (mine.astype(F32) + theirs.astype(F32)).astype(BF16)
    summed = summed.reshape(64, 4, 2, 256).transpose(0, 2, 1, 3).reshape(128, 8, 128)
    mixed = exchanged(summed, CHIP)
    mixed = mixed.reshape(128, 4, 8, 2, 2, 8).transpose(0, 1, 3, 4, 2, 5).reshape(128, 4, 256)
    tri_n = standardize_fn(mixed.astype(F32), 0).astype(BF16)
    out = jnp.einsum("crj,cz->rjz", tri_n, w_final, preferred_element_type=F32)
    own_n = standardize_fn(own.astype(F32), -1).astype(BF16)
    gate = jax.nn.sigmoid(jnp.einsum("rjz,zy->rjy", own_n, w_gate, preferred_element_type=F32))
    return (own.astype(F32) + gate * out).astype(BF16)


def solution(mesh):
    torus = Mesh(mesh.devices.reshape(2, 2, 2, 8, 2, 2), ("yh", "yl", "xl", "z", "core", "xh"))
    return jax.shard_map(
        per_device,
        mesh=torus,
        in_specs=(
            P(None, DAP, None),
            P(DAP, "xh", None),
            P(None, "xh"),
            P(),
            P("xh", None),
            P(),
            P(),
            P(),
        ),
        out_specs=P(DAP, "xh", None),
        check_vma=False,
    )
```

```python
import jax
import jax.numpy as jnp
from jax import lax
from jax.experimental import pallas as pl
from jax.experimental.pallas import tpu as pltpu
from jax.sharding import Mesh
from jax.sharding import PartitionSpec as P

DAP = ("yh", "yl", "xl", "z", "core")
PLANE = ("yl", "xl", "core")
CHIP = ("yh", "yl", "xl", "z", "xh")
F32 = jnp.float32
BF16 = jnp.bfloat16
VMEM = pl.BlockSpec(memory_space=pltpu.VMEM)
ANY = pl.BlockSpec(memory_space=pl.ANY)
SMEM = pl.BlockSpec(memory_space=pltpu.SMEM)


def dot(a, b, dims):
    return lax.dot_general(a, b, (dims, ((), ())), preferred_element_type=F32)


def standardized(x, axis):
    mean = jnp.mean(x, axis=axis, keepdims=True)
    centred = x - mean
    var = jnp.mean(centred * centred, axis=axis, keepdims=True)
    return centred * lax.rsqrt(var + 1e-05)


def on_core(kernel, outs, n_in, scratch=(), scalars=0, elsewhere=(), cost=None, limit=12):
    return pl.pallas_call(
        kernel,
        out_shape=outs,
        in_specs=[SMEM if i < scalars else ANY if i in elsewhere else VMEM for i in range(n_in)],
        out_specs=jax.tree.map(lambda _: VMEM, outs),
        scratch_shapes=scratch,
        compiler_params=pltpu.CompilerParams(vmem_limit_bytes=limit << 20),
        cost_estimate=cost,
    )


def cost(us):
    return pl.CostEstimate(flops=int(us * 1e9), bytes_accessed=int(us * 3e6), transcendentals=0)


def first_kernel(msa_ref, second_ref, right_ref, norm_ref):
    x = [msa_ref[:, i, :].astype(F32) for i in range(4)]
    for i in range(4):
        normed = standardized(x[i], -1).astype(BF16)
        norm_ref[i] = normed
        right_ref[i * 32 : (i + 1) * 32, :] = dot(second_ref[...], normed, ((0,), (1,))).astype(BF16)


def firsts(msa, second):
    return on_core(
        first_kernel,
        (jax.ShapeDtypeStruct((128, 128), BF16), jax.ShapeDtypeStruct((4, 128, 256), BF16)),
        2,
        cost=cost(1),
    )(msa, second)


def pack_kernel(me_ref, norm_ref, own_ref, other_ref, couple_ref, packed_ref):
    mex = me_ref[1]
    for i in range(4):
        normed = norm_ref[i]
        lo = dot(own_ref[...], normed, ((0,), (1,))).astype(BF16)
        hi = dot(other_ref[...], normed, ((0,), (1,))).astype(BF16)
        for g in range(8):
            packed_ref[g, pl.ds(pl.multiple_of(128 + mex * 64 + i * 16, 16), 16), :] = lo
            packed_ref[g, pl.ds(pl.multiple_of(192 - mex * 64 + i * 16, 16), 16), :] = hi
    row = lax.broadcasted_iota(jnp.int32, (8, 128), 0)
    for i in range(4):
        for y in range(4):
            for zz in range(4):
                pair = couple_ref[i, (y * 8 + zz * 2) * 8 : (y * 8 + zz * 2 + 2) * 8, :].astype(F32)
                a, b = pair[:8], pair[8:]
                rows = slice(i * 32 + zz * 8, i * 32 + zz * 8 + 8)
                packed_ref[y * 2, rows, :] = jnp.where(row < 4, a, pltpu.roll(b, 4, 0)).astype(BF16)
                packed_ref[y * 2 + 1, rows, :] = jnp.where(row < 4, pltpu.roll(a, 4, 0), b).astype(BF16)


def packs(me, normed, own, other, couple):
    return on_core(
        pack_kernel, jax.ShapeDtypeStruct((8, 256, 128), BF16), 5, scalars=1, cost=cost(1)
    )(me, normed, own, other, couple)


def wide_kernel(me_ref, own_ref, other_ref, wide_ref, w_scr):
    mex = me_ref[1]
    w_scr[pl.ds(pl.multiple_of(mex * 512, 512), 512), :] = own_ref[...].astype(F32)
    w_scr[pl.ds(pl.multiple_of(512 - mex * 512, 512), 512), :] = other_ref[...].astype(F32)
    wide_ref[...] = jnp.zeros_like(wide_ref)
    for e in range(32):
        w = w_scr[pl.ds(e, 32, stride=32), :].astype(BF16)
        for x in range(2):
            for i in range(4):
                row = ((e * 2 + x) * 4 + i) * 16
                wide_ref[row : row + 16, i * 128 : (i + 1) * 128] = w[x * 16 : (x + 1) * 16]


def widened(me, own, other):
    return on_core(
        wide_kernel,
        jax.ShapeDtypeStruct((4096, 512), BF16),
        3,
        [pltpu.VMEM((1024, 128), F32)],
        scalars=1,
        cost=cost(2),
    )(me, own, other)


def pair_kernel(me_ref, right_ref, packed_ref, wide_ref, entry_ref, *rest):
    lifted_refs, cols_ref = rest[:8], rest[8]
    rows_scr, lhs_scr, cols_scr, norm_scr, up_scr, wide_scr, sem = rest[9:]
    me = me_ref[0]
    fetch = pltpu.make_async_copy(wide_ref, wide_scr, sem)
    fetch.start()
    for z in range(8):
        for j in range(4):
            rows_scr[pl.ds(z * 4 + j, 32, stride=32), :] = right_ref[z, j * 32 : (j + 1) * 32, :].astype(F32)
    lefts = jnp.concatenate([packed_ref[g, 128:256, :] for g in range(8)], axis=0)
    for part in range(4):
        rows = rows_scr[part * 256 : (part + 1) * 256, :].astype(BF16)
        outer = (dot(rows, lefts, ((1,), (1,))) * (1.0 / 128)).astype(BF16)
        for e in range(8):
            for g in range(8):
                lhs_scr[g * 32 : (g + 1) * 32, (part * 8 + e) * 128 : (part * 8 + e + 1) * 128] = outer[
                    e * 32 : (e + 1) * 32, g * 128 : (g + 1) * 128
                ]
    fetch.wait()
    for half in range(2):
        rows = slice(half * 128, (half + 1) * 128)
        up_scr[rows, :] = dot(lhs_scr[rows, :], wide_scr[...], ((1,), (0,)))
    for m in range(8):
        g = m ^ me
        for i in range(4):
            lifted = (
                packed_ref[g, i * 32 : (i + 1) * 32, :].astype(F32)
                + up_scr[pl.ds(pl.multiple_of(g * 32, 32), 32), i * 128 : (i + 1) * 128]
            ).astype(BF16)
            lifted_refs[m][i * 32 : (i + 1) * 32, :] = lifted
            norm_scr[pl.ds(pl.multiple_of(g * 128 + i * 32, 32), 32), :] = standardized(
                lifted.astype(F32), -1
            ).astype(BF16)
    for g in range(8):
        normed = norm_scr[g * 128 : (g + 1) * 128, :]
        p = [dot(entry_ref[q], normed, ((1,), (1,))) for q in range(4)]
        cols_scr[pl.ds(g, 128, stride=16), :] = jax.nn.sigmoid(p[0]) * p[1]
        cols_scr[pl.ds(8 + g, 128, stride=16), :] = jax.nn.sigmoid(p[2]) * p[3]
    for part in range(8):
        cols_ref[part * 16 : (part + 1) * 16] = (
            cols_scr[part * 256 : (part + 1) * 256, :].reshape(16, 16, 128).astype(BF16)
        )


def pairs(me, right, packed, wide, entry_t):
    out = on_core(
        pair_kernel,
        (jax.ShapeDtypeStruct((128, 128), BF16),) * 8 + (jax.ShapeDtypeStruct((128, 16, 128), BF16),),
        5,
        [
            pltpu.VMEM((1024, 128), F32),
            pltpu.VMEM((256, 4096), BF16),
            pltpu.VMEM((2048, 128), F32),
            pltpu.VMEM((1024, 128), BF16),
            pltpu.VMEM((256, 512), F32),
            pltpu.VMEM((4096, 512), BF16),
            pltpu.SemaphoreType.DMA(()),
        ],
        elsewhere=(3,),
        limit=20,
        scalars=1,
        cost=cost(5),
    )(me, right, packed, wide, entry_t)
    return out[:8], out[8]


def regrouped(v, lane):
    low, even = lane < 64, (lane // 32) % 2 == 0
    t0 = jnp.where(low, v[0], pltpu.roll(v[2], 64, 1))
    t2 = jnp.where(low, pltpu.roll(v[0], 64, 1), v[2])
    t1 = jnp.where(low, v[1], pltpu.roll(v[3], 64, 1))
    t3 = jnp.where(low, pltpu.roll(v[1], 64, 1), v[3])
    u0 = jnp.where(even, t0, pltpu.roll(t1, 32, 1))
    u1 = jnp.where(even, pltpu.roll(t0, 96, 1), t1)
    u2 = jnp.where(even, t2, pltpu.roll(t3, 32, 1))
    u3 = jnp.where(even, pltpu.roll(t2, 96, 1), t3)
    return u0, u1, u2, u3


def product_kernel(me_ref, cols_ref, mine_ref, theirs_ref, ops_scr, out_scr):
    core = me_ref[2]
    lane = lax.broadcasted_iota(jnp.int32, (8, 128), 1)
    for yh in range(2):
        for z in range(8):
            for part in range(2):
                pieces = []
                for xh in range(2):
                    for x in range(2):
                        src = (((yh * 2 + part) * 2 + x) * 8 + z) * 2 + xh
                        pieces.append(cols_ref[src].astype(F32))
                left = regrouped([p[0:8] for p in pieces], lane)
                right = regrouped([p[8:16] for p in pieces], lane)
                lanes = slice(part * 128, (part + 1) * 128)
                for q in range(4):
                    row = (q * 16 + yh * 8 + z) * 8
                    ops_scr[0, row : row + 8, lanes] = left[q]
                    row = (yh * 32 + q * 8 + z) * 8
                    ops_scr[1, row : row + 8, lanes] = right[q]
    rights = ops_scr[1].astype(BF16)
    for q in range(4):
        prod = dot(ops_scr[0, q * 128 : (q + 1) * 128, :].astype(BF16), rights, ((1,), (1,)))
        for yh in range(2):
            for z in range(8):
                for t in range(4):
                    start = yh * 1024 + (z * 2 + t // 2) * 8 + q * 2 + t % 2
                    out_scr[pl.ds(start, 8, stride=128), :] = prod[
                        (yh * 8 + z) * 8 : (yh * 8 + z + 1) * 8, t * 128 : (t + 1) * 128
                    ]
    for y in range(8):
        rows = slice(y * 16, (y + 1) * 16)
        mine_ref[rows] = out_scr[pl.ds(pl.multiple_of((y * 2 + core) * 128, 128), 128), :].reshape(16, 8, 128)
        theirs_ref[rows] = (
            out_scr[pl.ds(pl.multiple_of((y * 2 + 1 - core) * 128, 128), 128), :].reshape(16, 8, 128).astype(BF16)
        )


def products(me, cols):
    return on_core(
        product_kernel,
        (jax.ShapeDtypeStruct((128, 8, 128), F32), jax.ShapeDtypeStruct((128, 8, 128), BF16)),
        2,
        [pltpu.VMEM((2, 512, 256), F32), pltpu.VMEM((2048, 128), F32)],
        scalars=1,
        cost=cost(3),
    )(me, cols)


def crossed(scr, out_row):
    row = lax.broadcasted_iota(jnp.int32, (8, 128), 0)
    res = []
    for m in range(4):
        a, b = scr[out_row + m * 8 : out_row + m * 8 + 8, :], scr[out_row + 32 + m * 8 : out_row + 40 + m * 8, :]
        res.append(jnp.where(row < 4, a, pltpu.roll(b, 4, 0)))
        res.append(jnp.where(row < 4, pltpu.roll(a, 4, 0), b))
    return jnp.concatenate(res, axis=0)


def gate_kernel(me_ref, *rest):
    own_refs, w_ref, gate_ref, base_ref, gate_scr, base_scr = rest[:8], *rest[8:]
    me = me_ref[0]
    for m in range(8):
        x = own_refs[m][...].astype(F32)
        normed = standardized(x, -1).astype(BF16)
        gate = jax.nn.sigmoid(dot(normed, w_ref[...], ((1,), (0,))))
        for i in range(4):
            rows = pl.ds(pl.multiple_of(i * 256 + (m ^ me) * 32, 32), 32)
            gate_scr[rows, :] = gate[i * 32 : (i + 1) * 32]
            base_scr[rows, :] = x[i * 32 : (i + 1) * 32]
    for b in range(16):
        gate_ref[b * 64 : (b + 1) * 64, :] = crossed(gate_scr, b * 64)
        base_ref[b * 64 : (b + 1) * 64, :] = crossed(base_scr, b * 64)


def gates(me, own, w):
    return on_core(
        gate_kernel,
        (jax.ShapeDtypeStruct((1024, 128), F32), jax.ShapeDtypeStruct((1024, 128), F32)),
        10,
        [pltpu.VMEM((1024, 128), F32), pltpu.VMEM((1024, 128), F32)],
        scalars=1,
        cost=cost(2),
    )(me, *own, w)


def final_kernel(mixed_ref, gate_ref, base_ref, w_ref, out_ref, norm_scr, mm_scr):
    tri_n = standardized(mixed_ref[...].astype(F32), 0)
    norm_scr[...] = tri_n.reshape(1024, 128)
    for i in range(4):
        for t in range(2):
            x = norm_scr[pl.ds(i * 2 + t, 128, stride=8), :].astype(BF16)
            out = dot(x, w_ref[...], ((0,), (0,)))
            for j in range(2):
                for z in range(8):
                    row = (j * 8 + z) * 8
                    mm_scr[pl.ds(i * 256 + z * 4 + t * 2 + j, 8, stride=32), :] = out[row : row + 8]
    for b in range(16):
        rows = slice(b * 64, (b + 1) * 64)
        out_ref[rows, :] = (base_ref[rows, :] + gate_ref[rows, :] * crossed(mm_scr, b * 64)).astype(BF16)


def finals(mixed, gate, base, w):
    return on_core(
        final_kernel,
        jax.ShapeDtypeStruct((1024, 128), BF16),
        4,
        [pltpu.VMEM((1024, 128), F32), pltpu.VMEM((1024, 128), F32)],
        cost=cost(2),
    )(mixed, gate, base, w)


def exchanged(x, axes):
    return lax.all_to_all(x, axes, split_axis=0, concat_axis=0, tiled=True)


def partner(x, axis):
    return lax.ppermute(x, axis, [(0, 1), (1, 0)])


def per_device(msa, couple, first, second, w_out, entry, w_gate, w_final):
    at = {name: lax.axis_index(name) for name in ("yh", "yl", "xl", "core", "xh")}
    me = jnp.stack([at["yl"] * 4 + at["xl"] * 2 + at["core"], at["xh"], at["core"]]).astype(jnp.int32)
    first_other = partner(first, "xh")
    w_other = partner(w_out, "xh")
    right, normed = firsts(msa, second)
    right = jnp.where(at["yh"] == at["xh"], right, partner(right, "yh"))
    packed = exchanged(packs(me, normed, first, first_other, couple), PLANE)
    right = exchanged(jnp.broadcast_to(right, (8, 128, 128)), "z")
    wide = widened(me, w_out, w_other)
    lifted, cols = pairs(me, right, packed, wide, jnp.swapaxes(entry, 1, 2))
    cols = exchanged(cols, CHIP)
    own = [lifted[0]]
    own += [lax.ppermute(lifted[m], PLANE, [(i, i ^ m) for i in range(8)]) for m in range(1, 8)]
    gate, base = gates(me, own, w_gate)
    mine, theirs = products(me, cols)
    summed = (mine + partner(theirs, "core").astype(F32)).astype(BF16)
    mixed = exchanged(summed, CHIP)
    return finals(mixed, gate, base, w_final).reshape(4, 256, 128)


def solution(mesh):
    torus = Mesh(mesh.devices.reshape(2, 2, 2, 8, 2, 2), ("yh", "yl", "xl", "z", "core", "xh"))
    return jax.shard_map(
        per_device,
        mesh=torus,
        in_specs=(
            P(None, DAP, None),
            P(DAP, "xh", None),
            P(None, "xh"),
            P(),
            P("xh", None),
            P(),
            P(),
            P(),
        ),
        out_specs=P(DAP, "xh", None),
        check_vma=False,
    )
```

```python
import jax
import jax.numpy as jnp
from jax import lax
from jax.experimental import pallas as pl
from jax.experimental.pallas import tpu as pltpu
from jax.sharding import Mesh
from jax.sharding import PartitionSpec as P

DAP = ("yh", "yl", "xl", "z", "core")
PLANE = ("yl", "xl", "core")
CHIP = ("yh", "yl", "xl", "z", "xh")
F32 = jnp.float32
BF16 = jnp.bfloat16
VMEM = pl.BlockSpec(memory_space=pltpu.VMEM)
SMEM = pl.BlockSpec(memory_space=pltpu.SMEM)


def dot(a, b, dims):
    return lax.dot_general(a, b, (dims, ((), ())), preferred_element_type=F32)


def standardized(x, axis):
    mean = jnp.mean(x, axis=axis, keepdims=True)
    centred = x - mean
    var = jnp.mean(centred * centred, axis=axis, keepdims=True)
    return centred * lax.rsqrt(var + 1e-05)


def on_core(kernel, outs, n_in, scratch=(), scalars=0, cost=None, limit=12):
    return pl.pallas_call(
        kernel,
        out_shape=outs,
        in_specs=[SMEM if i < scalars else VMEM for i in range(n_in)],
        out_specs=jax.tree.map(lambda _: VMEM, outs),
        scratch_shapes=scratch,
        compiler_params=pltpu.CompilerParams(vmem_limit_bytes=limit << 20),
        cost_estimate=cost,
    )


def cost(us):
    return pl.CostEstimate(flops=int(us * 1e9), bytes_accessed=int(us * 3e6), transcendentals=0)


def first_kernel(msa_ref, second_ref, right_ref, norm_ref):
    for i in range(4):
        normed = standardized(msa_ref[:, i, :].astype(F32), -1).astype(BF16)
        norm_ref[i] = normed
        right_ref[i * 32 : (i + 1) * 32, :] = dot(second_ref[...], normed, ((1,), (1,))).astype(BF16)


def firsts(msa, second_t):
    return on_core(
        first_kernel,
        (jax.ShapeDtypeStruct((128, 128), BF16), jax.ShapeDtypeStruct((4, 128, 256), BF16)),
        2,
        cost=cost(1),
    )(msa, second_t)


def spread_kernel(me_ref, own_ref, other_ref, all_ref):
    @pl.when(me_ref[3] == 1)
    def _():
        for z in range(8):
            all_ref[z] = own_ref[...]

    @pl.when(me_ref[3] == 0)
    def _():
        for z in range(8):
            all_ref[z] = other_ref[...]


def spreads(me, own, other):
    return on_core(
        spread_kernel, jax.ShapeDtypeStruct((8, 128, 128), BF16), 3, scalars=1, cost=cost(1)
    )(me, own, other)


def pack_kernel(me_ref, norm_ref, own_ref, other_ref, couple_ref, *packed_refs):
    me, mex = me_ref[0], me_ref[1]
    for i in range(4):
        normed = norm_ref[i]
        lo = dot(own_ref[...], normed, ((1,), (1,))).astype(BF16)
        hi = dot(other_ref[...], normed, ((1,), (1,))).astype(BF16)
        for m in range(8):
            packed_refs[m][pl.ds(pl.multiple_of(128 + mex * 64 + i * 16, 16), 16), :] = lo
            packed_refs[m][pl.ds(pl.multiple_of(192 - mex * 64 + i * 16, 16), 16), :] = hi
    row = lax.broadcasted_iota(jnp.int32, (8, 128), 0)
    for m in range(8):
        g = m ^ me
        keep = (row < 4) == (g % 2 == 0)
        for i in range(4):
            for zz in range(4):
                start = pl.multiple_of((g // 2) * 64 + zz * 16, 16)
                pair = couple_ref[i, pl.ds(start, 16), :].astype(F32)
                a, b = pair[:8], pair[8:]
                low = jnp.where(keep, a, pltpu.roll(a, 4, 0))
                high = jnp.where(keep, b, pltpu.roll(b, 4, 0))
                rows = slice(i * 32 + zz * 8, i * 32 + zz * 8 + 8)
                packed_refs[m][rows, :] = jnp.where(row < 4, low, high).astype(BF16)


def packs(me, normed, own_t, other_t, couple):
    return on_core(
        pack_kernel, (jax.ShapeDtypeStruct((256, 128), BF16),) * 8, 5, scalars=1, cost=cost(1)
    )(me, normed, own_t, other_t, couple)


def weight_kernel(me_ref, own_ref, other_ref, by_e_ref, w_scr):
    mex = me_ref[1]
    w_scr[pl.ds(pl.multiple_of(mex * 512, 512), 512), :] = own_ref[...].astype(F32)
    w_scr[pl.ds(pl.multiple_of(512 - mex * 512, 512), 512), :] = other_ref[...].astype(F32)
    for e in range(32):
        by_e_ref[e] = w_scr[pl.ds(e, 32, stride=32), :].astype(BF16)


def weights(me, own, other):
    return on_core(
        weight_kernel,
        jax.ShapeDtypeStruct((32, 32, 128), BF16),
        3,
        [pltpu.VMEM((1024, 128), F32)],
        scalars=1,
        cost=cost(1),
    )(me, own, other)


def pair_kernel(me_ref, right_ref, *rest):
    packed_refs, by_e_ref, entry_ref = rest[:8], rest[8], rest[9]
    lifted_refs, cols_ref = rest[10:18], rest[18]
    rows_scr, lhs_scr, cols_scr, wide_scr = rest[19:]
    me = me_ref[0]
    for z in range(8):
        for j in range(4):
            rows_scr[pl.ds(z * 4 + j, 32, stride=32), :] = right_ref[z, j * 32 : (j + 1) * 32, :].astype(F32)
    lefts = jnp.concatenate([packed_refs[m][128:256, :] for m in range(8)], axis=0)
    blank = jnp.zeros((16, 128), BF16)
    for part in range(4):
        for e in range(part * 8, part * 8 + 8):
            for x in range(2):
                for i in range(4):
                    for j in range(4):
                        row = ((e * 2 + x) * 4 + i) * 16
                        wide_scr[row : row + 16, j * 128 : (j + 1) * 128] = (
                            by_e_ref[e, x * 16 : (x + 1) * 16, :] if i == j else blank
                        )
        rows = rows_scr[part * 256 : (part + 1) * 256, :].astype(BF16)
        outer = (dot(rows, lefts, ((1,), (1,))) * (1.0 / 128)).astype(BF16)
        for e in range(8):
            for m in range(8):
                lhs_scr[m * 32 : (m + 1) * 32, (part * 8 + e) * 128 : (part * 8 + e + 1) * 128] = outer[
                    e * 32 : (e + 1) * 32, m * 128 : (m + 1) * 128
                ]
    for half in range(2):
        update = dot(lhs_scr[half * 128 : (half + 1) * 128, :], wide_scr[...], ((1,), (0,)))
        for mm in range(4):
            m = half * 4 + mm
            normed = []
            for i in range(4):
                rows = slice(i * 32, (i + 1) * 32)
                lifted = (
                    packed_refs[m][rows, :].astype(F32)
                    + update[mm * 32 : (mm + 1) * 32, i * 128 : (i + 1) * 128]
                ).astype(BF16)
                lifted_refs[m][rows, :] = lifted
                normed.append(standardized(lifted.astype(F32), -1).astype(BF16))
            normed = jnp.concatenate(normed, axis=0)
            p = [dot(entry_ref[q], normed, ((1,), (1,))) for q in range(4)]
            cols_scr[pl.ds(m ^ me, 128, stride=16), :] = jax.nn.sigmoid(p[0]) * p[1]
            cols_scr[pl.ds(8 + (m ^ me), 128, stride=16), :] = jax.nn.sigmoid(p[2]) * p[3]
    for part in range(8):
        cols_ref[part * 16 : (part + 1) * 16] = (
            cols_scr[part * 256 : (part + 1) * 256, :].reshape(16, 16, 128).astype(BF16)
        )


def pairs(me, right, packed, by_e, entry_t):
    out = on_core(
        pair_kernel,
        (jax.ShapeDtypeStruct((128, 128), BF16),) * 8 + (jax.ShapeDtypeStruct((128, 16, 128), BF16),),
        12,
        [
            pltpu.VMEM((1024, 128), F32),
            pltpu.VMEM((256, 4096), BF16),
            pltpu.VMEM((2048, 128), F32),
            pltpu.VMEM((4096, 512), BF16),
        ],
        scalars=1,
        limit=20,
        cost=cost(5),
    )(me, right, *packed, by_e, entry_t)
    return out[:8], out[8]


def regrouped(v, lane):
    low, even = lane < 64, (lane // 32) % 2 == 0
    t0 = jnp.where(low, v[0], pltpu.roll(v[2], 64, 1))
    t2 = jnp.where(low, pltpu.roll(v[0], 64, 1), v[2])
    t1 = jnp.where(low, v[1], pltpu.roll(v[3], 64, 1))
    t3 = jnp.where(low, pltpu.roll(v[1], 64, 1), v[3])
    u0 = jnp.where(even, t0, pltpu.roll(t1, 32, 1))
    u1 = jnp.where(even, pltpu.roll(t0, 96, 1), t1)
    u2 = jnp.where(even, t2, pltpu.roll(t3, 32, 1))
    u3 = jnp.where(even, pltpu.roll(t2, 96, 1), t3)
    return u0, u1, u2, u3


def product_kernel(me_ref, cols_ref, mine_ref, theirs_ref, ops_scr, out_scr):
    core = me_ref[2]
    lane = lax.broadcasted_iota(jnp.int32, (8, 128), 1)
    for yh in range(2):
        for z in range(8):
            for part in range(2):
                pieces = []
                for xh in range(2):
                    for x in range(2):
                        src = (((yh * 2 + part) * 2 + x) * 8 + z) * 2 + xh
                        pieces.append(cols_ref[src].astype(F32))
                left = regrouped([p[0:8] for p in pieces], lane)
                right = regrouped([p[8:16] for p in pieces], lane)
                lanes = slice(part * 128, (part + 1) * 128)
                for q in range(4):
                    row = (q * 16 + yh * 8 + z) * 8
                    ops_scr[0, row : row + 8, lanes] = left[q]
                    row = (yh * 32 + q * 8 + z) * 8
                    ops_scr[1, row : row + 8, lanes] = right[q]
    rights = ops_scr[1].astype(BF16)
    for q in range(4):
        prod = dot(ops_scr[0, q * 128 : (q + 1) * 128, :].astype(BF16), rights, ((1,), (1,)))
        for yh in range(2):
            for z in range(8):
                for t in range(4):
                    start = yh * 1024 + (z * 2 + t // 2) * 8 + q * 2 + t % 2
                    out_scr[pl.ds(start, 8, stride=128), :] = prod[
                        (yh * 8 + z) * 8 : (yh * 8 + z + 1) * 8, t * 128 : (t + 1) * 128
                    ]
    for y in range(8):
        rows = slice(y * 16, (y + 1) * 16)
        mine_ref[rows] = out_scr[pl.ds(pl.multiple_of((y * 2 + core) * 128, 128), 128), :].reshape(16, 8, 128)
        theirs_ref[rows] = (
            out_scr[pl.ds(pl.multiple_of((y * 2 + 1 - core) * 128, 128), 128), :].reshape(16, 8, 128).astype(BF16)
        )


def products(me, cols):
    return on_core(
        product_kernel,
        (jax.ShapeDtypeStruct((128, 8, 128), F32), jax.ShapeDtypeStruct((128, 8, 128), BF16)),
        2,
        [pltpu.VMEM((2, 512, 256), F32), pltpu.VMEM((2048, 128), F32)],
        scalars=1,
        cost=cost(3),
    )(me, cols)


def crossed(scr, out_row):
    row = lax.broadcasted_iota(jnp.int32, (8, 128), 0)
    res = []
    for m in range(4):
        a, b = scr[out_row + m * 8 : out_row + m * 8 + 8, :], scr[out_row + 32 + m * 8 : out_row + 40 + m * 8, :]
        res.append(jnp.where(row < 4, a, pltpu.roll(b, 4, 0)))
        res.append(jnp.where(row < 4, pltpu.roll(a, 4, 0), b))
    return jnp.concatenate(res, axis=0)


def gate_kernel(me_ref, *rest):
    own_refs, w_ref, gate_ref, base_ref, gate_scr, base_scr = rest[:8], *rest[8:]
    me = me_ref[0]
    for m in range(8):
        x = own_refs[m][...].astype(F32)
        normed = standardized(x, -1).astype(BF16)
        gate = jax.nn.sigmoid(dot(normed, w_ref[...], ((1,), (0,))))
        for i in range(4):
            rows = pl.ds(pl.multiple_of(i * 256 + (m ^ me) * 32, 32), 32)
            gate_scr[rows, :] = gate[i * 32 : (i + 1) * 32]
            base_scr[rows, :] = x[i * 32 : (i + 1) * 32]
    for b in range(16):
        gate_ref[b * 64 : (b + 1) * 64, :] = crossed(gate_scr, b * 64)
        base_ref[b * 64 : (b + 1) * 64, :] = crossed(base_scr, b * 64)


def gates(me, own, w):
    return on_core(
        gate_kernel,
        (jax.ShapeDtypeStruct((1024, 128), F32), jax.ShapeDtypeStruct((1024, 128), F32)),
        10,
        [pltpu.VMEM((1024, 128), F32), pltpu.VMEM((1024, 128), F32)],
        scalars=1,
        cost=cost(2),
    )(me, *own, w)


def final_kernel(mixed_ref, gate_ref, base_ref, w_ref, out_ref, norm_scr, mm_scr):
    tri_n = standardized(mixed_ref[...].astype(F32), 0)
    norm_scr[...] = tri_n.reshape(1024, 128)
    for i in range(4):
        for t in range(2):
            x = norm_scr[pl.ds(i * 2 + t, 128, stride=8), :].astype(BF16)
            out = dot(x, w_ref[...], ((0,), (0,)))
            for j in range(2):
                for z in range(8):
                    row = (j * 8 + z) * 8
                    mm_scr[pl.ds(i * 256 + z * 4 + t * 2 + j, 8, stride=32), :] = out[row : row + 8]
    for b in range(16):
        rows = slice(b * 64, (b + 1) * 64)
        out_ref[rows, :] = (base_ref[rows, :] + gate_ref[rows, :] * crossed(mm_scr, b * 64)).astype(BF16)


def finals(mixed, gate, base, w):
    return on_core(
        final_kernel,
        jax.ShapeDtypeStruct((1024, 128), BF16),
        4,
        [pltpu.VMEM((1024, 128), F32), pltpu.VMEM((1024, 128), F32)],
        cost=cost(2),
    )(mixed, gate, base, w)


def exchanged(x, axes):
    return lax.all_to_all(x, axes, split_axis=0, concat_axis=0, tiled=True)


def partner(x, axis):
    return lax.ppermute(x, axis, [(0, 1), (1, 0)])


def to_peers(pieces):
    sent = [lax.ppermute(pieces[m], PLANE, [(i, i ^ m) for i in range(8)]) for m in range(1, 8)]
    return [pieces[0], *sent]


def per_device(msa, couple, first, second, w_out, entry, w_gate, w_final):
    at = {name: lax.axis_index(name) for name in ("yh", "yl", "xl", "core", "xh")}
    me = jnp.stack(
        [at["yl"] * 4 + at["xl"] * 2 + at["core"], at["xh"], at["core"], (at["yh"] == at["xh"]).astype(jnp.int32)]
    ).astype(jnp.int32)
    right, normed = firsts(msa, second.T)
    first_t, w_out, right = lax.optimization_barrier((first.T, w_out, right))
    right = spreads(me, right, partner(right, "yh"))
    first_other = partner(first_t, "xh")
    w_other = partner(w_out, "xh")
    right, normed = lax.optimization_barrier((right, normed))
    right = exchanged(right, "z")
    packed = to_peers(packs(me, normed, first_t, first_other, couple))
    by_e = weights(me, w_out, w_other)
    lifted, cols = pairs(me, right, packed, by_e, jnp.swapaxes(entry, 1, 2))
    cols = exchanged(cols, CHIP)
    gate, base = gates(me, to_peers(lifted), w_gate)
    me, gate, base = lax.optimization_barrier((me, gate, base))
    mine, theirs = products(me, cols)
    summed = (mine + partner(theirs, "core").astype(F32)).astype(BF16)
    mixed = exchanged(summed, CHIP)
    return finals(mixed, gate, base, w_final).reshape(4, 256, 128)


def solution(mesh):
    torus = Mesh(mesh.devices.reshape(2, 2, 2, 8, 2, 2), ("yh", "yl", "xl", "z", "core", "xh"))
    return jax.shard_map(
        per_device,
        mesh=torus,
        in_specs=(
            P(None, DAP, None),
            P(DAP, "xh", None),
            P(None, "xh"),
            P(),
            P("xh", None),
            P(),
            P(),
            P(),
        ),
        out_specs=P(DAP, "xh", None),
        check_vma=False,
    )
```

```python
import jax
import jax.numpy as jnp
from jax import lax
from jax.experimental import pallas as pl
from jax.experimental.pallas import tpu as pltpu
from jax.sharding import Mesh
from jax.sharding import PartitionSpec as P

DAP = ("yh", "yl", "xl", "z", "core")
PLANE = ("yl", "xl", "core")
CHIP = ("yh", "yl", "xl", "z", "xh")
F32 = jnp.float32
BF16 = jnp.bfloat16
VMEM = pl.BlockSpec(memory_space=pltpu.VMEM)
SMEM = pl.BlockSpec(memory_space=pltpu.SMEM)


def dot(a, b, dims):
    return lax.dot_general(a, b, (dims, ((), ())), preferred_element_type=F32)


def standardized(x, axis):
    mean = jnp.mean(x, axis=axis, keepdims=True)
    centred = x - mean
    var = jnp.mean(centred * centred, axis=axis, keepdims=True)
    return centred * lax.rsqrt(var + 1e-05)


def on_core(kernel, outs, n_in, scratch=(), scalars=0, cost=None, limit=12):
    return pl.pallas_call(
        kernel,
        out_shape=outs,
        in_specs=[SMEM if i < scalars else VMEM for i in range(n_in)],
        out_specs=jax.tree.map(lambda _: VMEM, outs),
        scratch_shapes=scratch,
        compiler_params=pltpu.CompilerParams(vmem_limit_bytes=limit << 20),
        cost_estimate=cost,
    )


def cost(us):
    return pl.CostEstimate(flops=int(us * 1e9), bytes_accessed=int(us * 3e6), transcendentals=0)


def first_kernel(msa_ref, second_ref, right_ref, norm_ref):
    for i in range(4):
        normed = standardized(msa_ref[:, i, :].astype(F32), -1).astype(BF16)
        norm_ref[i] = normed
        right = dot(second_ref[...], normed, ((1,), (1,))).astype(BF16)
        for z in range(8):
            right_ref[z, i * 32 : (i + 1) * 32, :] = right


def firsts(msa, second_t):
    return on_core(
        first_kernel,
        (jax.ShapeDtypeStruct((8, 128, 128), BF16), jax.ShapeDtypeStruct((4, 128, 256), BF16)),
        2,
        cost=cost(1),
    )(msa, second_t)


def pack_kernel(me_ref, norm_ref, own_ref, other_ref, couple_ref, *packed_refs):
    me, mex = me_ref[0], me_ref[1]
    for i in range(4):
        normed = norm_ref[i]
        lo = dot(own_ref[...], normed, ((1,), (1,))).astype(BF16)
        hi = dot(other_ref[...], normed, ((1,), (1,))).astype(BF16)
        for m in range(8):
            packed_refs[m][pl.ds(pl.multiple_of(128 + mex * 64 + i * 16, 16), 16), :] = lo
            packed_refs[m][pl.ds(pl.multiple_of(192 - mex * 64 + i * 16, 16), 16), :] = hi
    row = lax.broadcasted_iota(jnp.int32, (8, 128), 0)
    for m in range(8):
        g = m ^ me
        keep = (row < 4) == (g % 2 == 0)
        for i in range(4):
            for zz in range(4):
                start = pl.multiple_of((g // 2) * 64 + zz * 16, 16)
                pair = couple_ref[i, pl.ds(start, 16), :].astype(F32)
                a, b = pair[:8], pair[8:]
                low = jnp.where(keep, a, pltpu.roll(a, 4, 0))
                high = jnp.where(keep, b, pltpu.roll(b, 4, 0))
                rows = slice(i * 32 + zz * 8, i * 32 + zz * 8 + 8)
                packed_refs[m][rows, :] = jnp.where(row < 4, low, high).astype(BF16)


def packs(me, normed, own_t, other_t, couple):
    return on_core(
        pack_kernel, (jax.ShapeDtypeStruct((256, 128), BF16),) * 8, 5, scalars=1, cost=cost(1)
    )(me, normed, own_t, other_t, couple)


def weight_kernel(me_ref, own_ref, other_ref, by_e_ref, w_scr):
    mex = me_ref[1]
    w_scr[pl.ds(pl.multiple_of(mex * 512, 512), 512), :] = own_ref[...].astype(F32)
    w_scr[pl.ds(pl.multiple_of(512 - mex * 512, 512), 512), :] = other_ref[...].astype(F32)
    for e in range(32):
        by_e_ref[e] = w_scr[pl.ds(e, 32, stride=32), :].astype(BF16)


def weights(me, own, other):
    return on_core(
        weight_kernel,
        jax.ShapeDtypeStruct((32, 32, 128), BF16),
        3,
        [pltpu.VMEM((1024, 128), F32)],
        scalars=1,
        cost=cost(1),
    )(me, own, other)


def pair_kernel(me_ref, own_ref, other_ref, *rest):
    packed_refs, by_e_ref, entry_ref = rest[:8], rest[8], rest[9]
    lifted_refs, cols_ref = rest[10:18], rest[18]
    rows_scr, lhs_scr, cols_scr, wide_scr = rest[19:]
    me = me_ref[0]
    keep = me_ref[3] == 1
    for z in range(8):
        for j in range(4):
            rows = slice(j * 32, (j + 1) * 32)
            rows_scr[pl.ds(z * 4 + j, 32, stride=32), :] = jnp.where(
                keep, own_ref[z, rows, :].astype(F32), other_ref[z, rows, :].astype(F32)
            )
    lefts = jnp.concatenate([packed_refs[m][128:256, :] for m in range(8)], axis=0)
    blank = jnp.zeros((16, 128), BF16)
    for part in range(4):
        for e in range(part * 8, part * 8 + 8):
            for x in range(2):
                for i in range(4):
                    for j in range(4):
                        row = ((e * 2 + x) * 4 + i) * 16
                        wide_scr[row : row + 16, j * 128 : (j + 1) * 128] = (
                            by_e_ref[e, x * 16 : (x + 1) * 16, :] if i == j else blank
                        )
        rows = rows_scr[part * 256 : (part + 1) * 256, :].astype(BF16)
        outer = (dot(rows, lefts, ((1,), (1,))) * (1.0 / 128)).astype(BF16)
        for e in range(8):
            for m in range(8):
                lhs_scr[m * 32 : (m + 1) * 32, (part * 8 + e) * 128 : (part * 8 + e + 1) * 128] = outer[
                    e * 32 : (e + 1) * 32, m * 128 : (m + 1) * 128
                ]
    for half in range(2):
        update = dot(lhs_scr[half * 128 : (half + 1) * 128, :], wide_scr[...], ((1,), (0,)))
        for mm in range(4):
            m = half * 4 + mm
            normed = []
            for i in range(4):
                rows = slice(i * 32, (i + 1) * 32)
                lifted = (
                    packed_refs[m][rows, :].astype(F32)
                    + update[mm * 32 : (mm + 1) * 32, i * 128 : (i + 1) * 128]
                ).astype(BF16)
                lifted_refs[m][rows, :] = lifted
                normed.append(standardized(lifted.astype(F32), -1).astype(BF16))
            normed = jnp.concatenate(normed, axis=0)
            p = [dot(entry_ref[q], normed, ((1,), (1,))) for q in range(4)]
            cols_scr[pl.ds(m ^ me, 128, stride=16), :] = jax.nn.sigmoid(p[0]) * p[1]
            cols_scr[pl.ds(8 + (m ^ me), 128, stride=16), :] = jax.nn.sigmoid(p[2]) * p[3]
    for part in range(8):
        cols_ref[part * 16 : (part + 1) * 16] = (
            cols_scr[part * 256 : (part + 1) * 256, :].reshape(16, 16, 128).astype(BF16)
        )


def pairs(me, right, other, packed, by_e, entry_t):
    out = on_core(
        pair_kernel,
        (jax.ShapeDtypeStruct((128, 128), BF16),) * 8 + (jax.ShapeDtypeStruct((128, 16, 128), BF16),),
        13,
        [
            pltpu.VMEM((1024, 128), F32),
            pltpu.VMEM((256, 4096), BF16),
            pltpu.VMEM((2048, 128), F32),
            pltpu.VMEM((4096, 512), BF16),
        ],
        scalars=1,
        limit=20,
        cost=cost(5),
    )(me, right, other, *packed, by_e, entry_t)
    return out[:8], out[8]


def regrouped(v, lane):
    low, even = lane < 64, (lane // 32) % 2 == 0
    t0 = jnp.where(low, v[0], pltpu.roll(v[2], 64, 1))
    t2 = jnp.where(low, pltpu.roll(v[0], 64, 1), v[2])
    t1 = jnp.where(low, v[1], pltpu.roll(v[3], 64, 1))
    t3 = jnp.where(low, pltpu.roll(v[1], 64, 1), v[3])
    u0 = jnp.where(even, t0, pltpu.roll(t1, 32, 1))
    u1 = jnp.where(even, pltpu.roll(t0, 96, 1), t1)
    u2 = jnp.where(even, t2, pltpu.roll(t3, 32, 1))
    u3 = jnp.where(even, pltpu.roll(t2, 96, 1), t3)
    return u0, u1, u2, u3


def product_kernel(me_ref, cols_ref, mine_ref, theirs_ref, ops_scr, out_scr):
    core = me_ref[2]
    lane = lax.broadcasted_iota(jnp.int32, (8, 128), 1)
    for yh in range(2):
        for z in range(8):
            for part in range(2):
                pieces = []
                for xh in range(2):
                    for x in range(2):
                        src = (((yh * 2 + part) * 2 + x) * 8 + z) * 2 + xh
                        pieces.append(cols_ref[src].astype(F32))
                left = regrouped([p[0:8] for p in pieces], lane)
                right = regrouped([p[8:16] for p in pieces], lane)
                lanes = slice(part * 128, (part + 1) * 128)
                for q in range(4):
                    row = (q * 16 + yh * 8 + z) * 8
                    ops_scr[0, row : row + 8, lanes] = left[q]
                    row = (yh * 32 + q * 8 + z) * 8
                    ops_scr[1, row : row + 8, lanes] = right[q]
    rights = ops_scr[1].astype(BF16)
    for q in range(4):
        prod = dot(ops_scr[0, q * 128 : (q + 1) * 128, :].astype(BF16), rights, ((1,), (1,)))
        for yh in range(2):
            for z in range(8):
                for t in range(4):
                    start = yh * 1024 + (z * 2 + t // 2) * 8 + q * 2 + t % 2
                    out_scr[pl.ds(start, 8, stride=128), :] = prod[
                        (yh * 8 + z) * 8 : (yh * 8 + z + 1) * 8, t * 128 : (t + 1) * 128
                    ]
    for y in range(8):
        rows = slice(y * 16, (y + 1) * 16)
        mine_ref[rows] = out_scr[pl.ds(pl.multiple_of((y * 2 + core) * 128, 128), 128), :].reshape(16, 8, 128)
        theirs_ref[rows] = (
            out_scr[pl.ds(pl.multiple_of((y * 2 + 1 - core) * 128, 128), 128), :].reshape(16, 8, 128).astype(BF16)
        )


def products(me, cols):
    return on_core(
        product_kernel,
        (jax.ShapeDtypeStruct((128, 8, 128), F32), jax.ShapeDtypeStruct((128, 8, 128), BF16)),
        2,
        [pltpu.VMEM((2, 512, 256), F32), pltpu.VMEM((2048, 128), F32)],
        scalars=1,
        cost=cost(3),
    )(me, cols)


def crossed(scr, out_row):
    row = lax.broadcasted_iota(jnp.int32, (8, 128), 0)
    res = []
    for m in range(4):
        a, b = scr[out_row + m * 8 : out_row + m * 8 + 8, :], scr[out_row + 32 + m * 8 : out_row + 40 + m * 8, :]
        res.append(jnp.where(row < 4, a, pltpu.roll(b, 4, 0)))
        res.append(jnp.where(row < 4, pltpu.roll(a, 4, 0), b))
    return jnp.concatenate(res, axis=0)


def gate_kernel(me_ref, *rest):
    own_refs, w_ref, gate_ref, base_ref, gate_scr, base_scr = rest[:8], *rest[8:]
    me = me_ref[0]
    for m in range(8):
        x = own_refs[m][...].astype(F32)
        normed = standardized(x, -1).astype(BF16)
        gate = jax.nn.sigmoid(dot(normed, w_ref[...], ((1,), (0,))))
        for i in range(4):
            rows = pl.ds(pl.multiple_of(i * 256 + (m ^ me) * 32, 32), 32)
            gate_scr[rows, :] = gate[i * 32 : (i + 1) * 32]
            base_scr[rows, :] = x[i * 32 : (i + 1) * 32]
    for b in range(16):
        gate_ref[b * 64 : (b + 1) * 64, :] = crossed(gate_scr, b * 64)
        base_ref[b * 64 : (b + 1) * 64, :] = crossed(base_scr, b * 64)


def gates(me, own, w):
    return on_core(
        gate_kernel,
        (jax.ShapeDtypeStruct((1024, 128), F32), jax.ShapeDtypeStruct((1024, 128), F32)),
        10,
        [pltpu.VMEM((1024, 128), F32), pltpu.VMEM((1024, 128), F32)],
        scalars=1,
        cost=cost(2),
    )(me, *own, w)


def final_kernel(mixed_ref, gate_ref, base_ref, w_ref, out_ref, norm_scr, mm_scr):
    tri_n = standardized(mixed_ref[...].astype(F32), 0)
    norm_scr[...] = tri_n.reshape(1024, 128)
    for i in range(4):
        for t in range(2):
            x = norm_scr[pl.ds(i * 2 + t, 128, stride=8), :].astype(BF16)
            out = dot(x, w_ref[...], ((0,), (0,)))
            for j in range(2):
                for z in range(8):
                    row = (j * 8 + z) * 8
                    mm_scr[pl.ds(i * 256 + z * 4 + t * 2 + j, 8, stride=32), :] = out[row : row + 8]
    for b in range(16):
        rows = slice(b * 64, (b + 1) * 64)
        out_ref[rows, :] = (base_ref[rows, :] + gate_ref[rows, :] * crossed(mm_scr, b * 64)).astype(BF16)


def finals(mixed, gate, base, w):
    return on_core(
        final_kernel,
        jax.ShapeDtypeStruct((1024, 128), BF16),
        4,
        [pltpu.VMEM((1024, 128), F32), pltpu.VMEM((1024, 128), F32)],
        cost=cost(2),
    )(mixed, gate, base, w)


def exchanged(x, axes):
    return lax.all_to_all(x, axes, split_axis=0, concat_axis=0, tiled=True)


def partner(x, axis):
    return lax.ppermute(x, axis, [(0, 1), (1, 0)])


def to_peers(pieces):
    sent = [lax.ppermute(pieces[m], PLANE, [(i, i ^ m) for i in range(8)]) for m in range(1, 8)]
    return [pieces[0], *sent]


def per_device(msa, couple, first, second, w_out, entry, w_gate, w_final):
    at = {name: lax.axis_index(name) for name in ("yh", "yl", "xl", "core", "xh")}
    me = jnp.stack(
        [at["yl"] * 4 + at["xl"] * 2 + at["core"], at["xh"], at["core"], (at["yh"] == at["xh"]).astype(jnp.int32)]
    ).astype(jnp.int32)
    right, normed = firsts(msa, second.T)
    first_t, w_out, right, normed = lax.optimization_barrier((first.T, w_out, right, normed))
    right = exchanged(right, "z")
    first_other = partner(first_t, "xh")
    w_other = partner(w_out, "xh")
    packed = packs(me, normed, first_t, first_other, couple)
    right, packed = lax.optimization_barrier((right, packed))
    other = partner(right, "yh")
    packed = to_peers(packed)
    by_e = weights(me, w_out, w_other)
    lifted, cols = pairs(me, right, other, packed, by_e, jnp.swapaxes(entry, 1, 2))
    cols = exchanged(cols, CHIP)
    gate, base = gates(me, to_peers(lifted), w_gate)
    me, gate, base = lax.optimization_barrier((me, gate, base))
    mine, theirs = products(me, cols)
    summed = (mine + partner(theirs, "core").astype(F32)).astype(BF16)
    mixed = exchanged(summed, CHIP)
    return finals(mixed, gate, base, w_final).reshape(4, 256, 128)


def solution(mesh):
    torus = Mesh(mesh.devices.reshape(2, 2, 2, 8, 2, 2), ("yh", "yl", "xl", "z", "core", "xh"))
    return jax.shard_map(
        per_device,
        mesh=torus,
        in_specs=(
            P(None, DAP, None),
            P(DAP, "xh", None),
            P(None, "xh"),
            P(),
            P("xh", None),
            P(),
            P(),
            P(),
        ),
        out_specs=P(DAP, "xh", None),
        check_vma=False,
    )
```

```python
import jax
import jax.numpy as jnp
from jax import lax
from jax.experimental import pallas as pl
from jax.experimental.pallas import tpu as pltpu
from jax.sharding import Mesh
from jax.sharding import PartitionSpec as P

DAP = ("yh", "yl", "xl", "z", "core")
PLANE = ("yl", "xl", "core")
CHIP = ("yh", "yl", "xl", "z", "xh")
F32 = jnp.float32
BF16 = jnp.bfloat16
VMEM = pl.BlockSpec(memory_space=pltpu.VMEM)
SMEM = pl.BlockSpec(memory_space=pltpu.SMEM)


def dot(a, b, dims):
    return lax.dot_general(a, b, (dims, ((), ())), preferred_element_type=F32)


def standardized(x, axis):
    mean = jnp.mean(x, axis=axis, keepdims=True)
    centred = x - mean
    var = jnp.mean(centred * centred, axis=axis, keepdims=True)
    return centred * lax.rsqrt(var + 1e-05)


def on_core(kernel, outs, n_in, scratch=(), scalars=0, cost=None, limit=12):
    return pl.pallas_call(
        kernel,
        out_shape=outs,
        in_specs=[SMEM if i < scalars else VMEM for i in range(n_in)],
        out_specs=jax.tree.map(lambda _: VMEM, outs),
        scratch_shapes=scratch,
        compiler_params=pltpu.CompilerParams(vmem_limit_bytes=limit << 20),
        cost_estimate=cost,
    )


def cost(us):
    return pl.CostEstimate(flops=int(us * 1e9), bytes_accessed=int(us * 3e6), transcendentals=0)


def first_kernel(msa_ref, second_ref, right_ref, norm_ref):
    for i in range(4):
        normed = standardized(msa_ref[:, i, :].astype(F32), -1).astype(BF16)
        norm_ref[i] = normed
        right = dot(second_ref[...], normed, ((1,), (1,))).astype(BF16)
        for z in range(16):
            right_ref[z, i * 32 : (i + 1) * 32, :] = right


def firsts(msa, second_t):
    return on_core(
        first_kernel,
        (jax.ShapeDtypeStruct((16, 128, 128), BF16), jax.ShapeDtypeStruct((4, 128, 256), BF16)),
        2,
        cost=cost(1),
    )(msa, second_t)


def pack_kernel(me_ref, norm_ref, own_ref, other_ref, couple_ref, *packed_refs):
    me, mex = me_ref[0], me_ref[1]
    for i in range(4):
        normed = norm_ref[i]
        lo = dot(own_ref[...], normed, ((1,), (1,))).astype(BF16)
        hi = dot(other_ref[...], normed, ((1,), (1,))).astype(BF16)
        for m in range(8):
            packed_refs[m][pl.ds(pl.multiple_of(128 + i * 32 + mex * 16, 16), 16), :] = lo
            packed_refs[m][pl.ds(pl.multiple_of(144 + i * 32 - mex * 16, 16), 16), :] = hi
    row = lax.broadcasted_iota(jnp.int32, (8, 128), 0)
    for m in range(8):
        g = m ^ me
        keep = (row < 4) == (g % 2 == 0)
        for i in range(4):
            for zz in range(4):
                start = pl.multiple_of((g // 2) * 64 + zz * 16, 16)
                pair = couple_ref[i, pl.ds(start, 16), :].astype(F32)
                a, b = pair[:8], pair[8:]
                low = jnp.where(keep, a, pltpu.roll(a, 4, 0))
                high = jnp.where(keep, b, pltpu.roll(b, 4, 0))
                rows = slice(i * 32 + zz * 8, i * 32 + zz * 8 + 8)
                packed_refs[m][rows, :] = jnp.where(row < 4, low, high).astype(BF16)


def packs(me, normed, own_t, other_t, couple):
    return on_core(
        pack_kernel, (jax.ShapeDtypeStruct((256, 128), BF16),) * 8, 5, scalars=1, cost=cost(1)
    )(me, normed, own_t, other_t, couple)


def weight_kernel(me_ref, own_ref, other_ref, wide_ref, w_scr):
    mex = me_ref[1]
    w_scr[pl.ds(pl.multiple_of(mex * 512, 512), 512), :] = own_ref[...].astype(F32)
    w_scr[pl.ds(pl.multiple_of(512 - mex * 512, 512), 512), :] = other_ref[...].astype(F32)
    blank = jnp.zeros((32, 128), BF16)
    for e in range(32):
        w = w_scr[pl.ds(e, 32, stride=32), :].astype(BF16)
        wide_ref[e * 64 : e * 64 + 32, 0:128] = w
        wide_ref[e * 64 : e * 64 + 32, 128:256] = blank
        wide_ref[e * 64 + 32 : e * 64 + 64, 0:128] = blank
        wide_ref[e * 64 + 32 : e * 64 + 64, 128:256] = w


def weights(me, own, other):
    return on_core(
        weight_kernel,
        jax.ShapeDtypeStruct((2048, 256), BF16),
        3,
        [pltpu.VMEM((1024, 128), F32)],
        scalars=1,
        cost=cost(1),
    )(me, own, other)


def pair_kernel(me_ref, right_ref, *rest):
    packed_refs, wide_ref, entry_ref = rest[:8], rest[8], rest[9]
    lifted_refs, cols_ref = rest[10:18], rest[18]
    rows_scr, lhs_scr, cols_scr = rest[19:]
    me = me_ref[0]
    for z in range(8):
        for j in range(4):
            rows_scr[pl.ds(z * 4 + j, 32, stride=32), :] = right_ref[
                me_ref[1] * 8 + z, j * 32 : (j + 1) * 32, :
            ].astype(F32)
    lefts = jnp.concatenate([packed_refs[m][128:256, :] for m in range(8)], axis=0)
    low = lax.broadcasted_iota(jnp.int32, (32, 128), 1) < 64
    for part in range(4):
        rows = rows_scr[part * 256 : (part + 1) * 256, :].astype(BF16)
        outer = dot(rows, lefts, ((1,), (1,))) * (1.0 / 128)
        for e in range(4):
            for m in range(8):
                lanes = slice(m * 128, (m + 1) * 128)
                a = outer[e * 64 : e * 64 + 32, lanes]
                b = outer[e * 64 + 32 : e * 64 + 64, lanes]
                rows = slice(m * 32, (m + 1) * 32)
                at = slice((part * 4 + e) * 128, (part * 4 + e + 1) * 128)
                lhs_scr[0, rows, at] = jnp.where(low, a, pltpu.roll(b, 64, 1)).astype(BF16)
                lhs_scr[1, rows, at] = jnp.where(low, pltpu.roll(a, 64, 1), b).astype(BF16)
    for half in range(2):
        update = [
            dot(lhs_scr[p, half * 128 : (half + 1) * 128, :], wide_ref[...], ((1,), (0,))) for p in range(2)
        ]
        for mm in range(4):
            m = half * 4 + mm
            normed = []
            for i in range(4):
                rows = slice(i * 32, (i + 1) * 32)
                lifted = (
                    packed_refs[m][rows, :].astype(F32)
                    + update[i // 2][mm * 32 : (mm + 1) * 32, (i % 2) * 128 : (i % 2 + 1) * 128]
                ).astype(BF16)
                lifted_refs[m][rows, :] = lifted
                normed.append(standardized(lifted.astype(F32), -1).astype(BF16))
            normed = jnp.concatenate(normed, axis=0)
            p = [dot(entry_ref[q], normed, ((1,), (1,))) for q in range(4)]
            cols_scr[pl.ds(m ^ me, 128, stride=16), :] = jax.nn.sigmoid(p[0]) * p[1]
            cols_scr[pl.ds(8 + (m ^ me), 128, stride=16), :] = jax.nn.sigmoid(p[2]) * p[3]
    for part in range(8):
        cols_ref[part * 16 : (part + 1) * 16] = (
            cols_scr[part * 256 : (part + 1) * 256, :].reshape(16, 16, 128).astype(BF16)
        )


def pairs(me, right, packed, by_e, entry_t):
    out = on_core(
        pair_kernel,
        (jax.ShapeDtypeStruct((128, 128), BF16),) * 8 + (jax.ShapeDtypeStruct((128, 16, 128), BF16),),
        12,
        [
            pltpu.VMEM((1024, 128), F32),
            pltpu.VMEM((2, 256, 2048), BF16),
            pltpu.VMEM((2048, 128), F32),
        ],
        scalars=1,
        limit=14,
        cost=cost(5),
    )(me, right, *packed, by_e, entry_t)
    return out[:8], out[8]


def regrouped(v, lane):
    low, even = lane < 64, (lane // 32) % 2 == 0
    t0 = jnp.where(low, v[0], pltpu.roll(v[2], 64, 1))
    t2 = jnp.where(low, pltpu.roll(v[0], 64, 1), v[2])
    t1 = jnp.where(low, v[1], pltpu.roll(v[3], 64, 1))
    t3 = jnp.where(low, pltpu.roll(v[1], 64, 1), v[3])
    u0 = jnp.where(even, t0, pltpu.roll(t1, 32, 1))
    u1 = jnp.where(even, pltpu.roll(t0, 96, 1), t1)
    u2 = jnp.where(even, t2, pltpu.roll(t3, 32, 1))
    u3 = jnp.where(even, pltpu.roll(t2, 96, 1), t3)
    return u0, u1, u2, u3


def product_kernel(me_ref, cols_ref, mine_ref, theirs_ref, ops_scr, out_scr):
    core = me_ref[2]
    lane = lax.broadcasted_iota(jnp.int32, (8, 128), 1)
    for yh in range(2):
        for z in range(8):
            for part in range(2):
                pieces = []
                for xh in range(2):
                    for x in range(2):
                        src = (((yh * 2 + part) * 2 + x) * 8 + z) * 2 + xh
                        pieces.append(cols_ref[src].astype(F32))
                left = regrouped([p[0:8] for p in pieces], lane)
                right = regrouped([p[8:16] for p in pieces], lane)
                lanes = slice(part * 128, (part + 1) * 128)
                for q in range(4):
                    row = (q * 16 + yh * 8 + z) * 8
                    ops_scr[0, row : row + 8, lanes] = left[q]
                    row = (yh * 32 + q * 8 + z) * 8
                    ops_scr[1, row : row + 8, lanes] = right[q]
    rights = ops_scr[1].astype(BF16)
    for q in range(4):
        prod = dot(ops_scr[0, q * 128 : (q + 1) * 128, :].astype(BF16), rights, ((1,), (1,)))
        for yh in range(2):
            for z in range(8):
                for t in range(4):
                    start = yh * 1024 + (z * 2 + t // 2) * 8 + q * 2 + t % 2
                    out_scr[pl.ds(start, 8, stride=128), :] = prod[
                        (yh * 8 + z) * 8 : (yh * 8 + z + 1) * 8, t * 128 : (t + 1) * 128
                    ]
    for y in range(8):
        rows = slice(y * 16, (y + 1) * 16)
        mine_ref[rows] = out_scr[pl.ds(pl.multiple_of((y * 2 + core) * 128, 128), 128), :].reshape(16, 8, 128)
        theirs_ref[rows] = (
            out_scr[pl.ds(pl.multiple_of((y * 2 + 1 - core) * 128, 128), 128), :].reshape(16, 8, 128).astype(BF16)
        )


def products(me, cols):
    return on_core(
        product_kernel,
        (jax.ShapeDtypeStruct((128, 8, 128), F32), jax.ShapeDtypeStruct((128, 8, 128), BF16)),
        2,
        [pltpu.VMEM((2, 512, 256), F32), pltpu.VMEM((2048, 128), F32)],
        scalars=1,
        cost=cost(3),
    )(me, cols)


def crossed(scr, out_row):
    row = lax.broadcasted_iota(jnp.int32, (8, 128), 0)
    res = []
    for m in range(4):
        a, b = scr[out_row + m * 8 : out_row + m * 8 + 8, :], scr[out_row + 32 + m * 8 : out_row + 40 + m * 8, :]
        res.append(jnp.where(row < 4, a, pltpu.roll(b, 4, 0)))
        res.append(jnp.where(row < 4, pltpu.roll(a, 4, 0), b))
    return jnp.concatenate(res, axis=0)


def gate_kernel(me_ref, *rest):
    own_refs, w_ref, gate_ref, base_ref, gate_scr, base_scr = rest[:8], *rest[8:]
    me = me_ref[0]
    for m in range(8):
        x = own_refs[m][...].astype(F32)
        normed = standardized(x, -1).astype(BF16)
        gate = jax.nn.sigmoid(dot(normed, w_ref[...], ((1,), (0,))))
        for i in range(4):
            rows = pl.ds(pl.multiple_of(i * 256 + (m ^ me) * 32, 32), 32)
            gate_scr[rows, :] = gate[i * 32 : (i + 1) * 32]
            base_scr[rows, :] = x[i * 32 : (i + 1) * 32]
    for b in range(16):
        gate_ref[b * 64 : (b + 1) * 64, :] = crossed(gate_scr, b * 64)
        base_ref[b * 64 : (b + 1) * 64, :] = crossed(base_scr, b * 64)


def gates(me, own, w):
    return on_core(
        gate_kernel,
        (jax.ShapeDtypeStruct((1024, 128), F32), jax.ShapeDtypeStruct((1024, 128), F32)),
        10,
        [pltpu.VMEM((1024, 128), F32), pltpu.VMEM((1024, 128), F32)],
        scalars=1,
        cost=cost(2),
    )(me, *own, w)


def final_kernel(mixed_ref, gate_ref, base_ref, w_ref, out_ref, norm_scr, mm_scr):
    tri_n = standardized(mixed_ref[...].astype(F32), 0)
    norm_scr[...] = tri_n.reshape(1024, 128)
    for i in range(4):
        for t in range(2):
            x = norm_scr[pl.ds(i * 2 + t, 128, stride=8), :].astype(BF16)
            out = dot(x, w_ref[...], ((0,), (0,)))
            for j in range(2):
                for z in range(8):
                    row = (j * 8 + z) * 8
                    mm_scr[pl.ds(i * 256 + z * 4 + t * 2 + j, 8, stride=32), :] = out[row : row + 8]
    for b in range(16):
        rows = slice(b * 64, (b + 1) * 64)
        out_ref[rows, :] = (base_ref[rows, :] + gate_ref[rows, :] * crossed(mm_scr, b * 64)).astype(BF16)


def finals(mixed, gate, base, w):
    return on_core(
        final_kernel,
        jax.ShapeDtypeStruct((1024, 128), BF16),
        4,
        [pltpu.VMEM((1024, 128), F32), pltpu.VMEM((1024, 128), F32)],
        cost=cost(2),
    )(mixed, gate, base, w)


def exchanged(x, axes):
    return lax.all_to_all(x, axes, split_axis=0, concat_axis=0, tiled=True)


def partner(x, axis):
    return lax.ppermute(x, axis, [(0, 1), (1, 0)])


def to_peers(pieces):
    sent = [lax.ppermute(pieces[m], PLANE, [(i, i ^ m) for i in range(8)]) for m in range(1, 8)]
    return [pieces[0], *sent]


def per_device(msa, couple, first, second, w_out, entry, w_gate, w_final):
    at = {name: lax.axis_index(name) for name in ("yh", "yl", "xl", "core", "xh")}
    me = jnp.stack(
        [at["yl"] * 4 + at["xl"] * 2 + at["core"], at["xh"], at["core"], (at["yh"] == at["xh"]).astype(jnp.int32)]
    ).astype(jnp.int32)
    right, normed = firsts(msa, second.T)
    first_t, w_out, right, normed = lax.optimization_barrier((first.T, w_out, right, normed))
    right = exchanged(right, ("yh", "z"))
    first_other = partner(first_t, "xh")
    w_other = partner(w_out, "xh")
    packed = to_peers(packs(me, normed, first_t, first_other, couple))
    by_e = weights(me, w_out, w_other)
    lifted, cols = pairs(me, right, packed, by_e, jnp.swapaxes(entry, 1, 2))
    cols = exchanged(cols, CHIP)
    gate, base = gates(me, to_peers(lifted), w_gate)
    me, gate, base = lax.optimization_barrier((me, gate, base))
    mine, theirs = products(me, cols)
    summed = (mine + partner(theirs, "core").astype(F32)).astype(BF16)
    mixed = exchanged(summed, CHIP)
    return finals(mixed, gate, base, w_final).reshape(4, 256, 128)


def solution(mesh):
    torus = Mesh(mesh.devices.reshape(2, 2, 2, 8, 2, 2), ("yh", "yl", "xl", "z", "core", "xh"))
    return jax.shard_map(
        per_device,
        mesh=torus,
        in_specs=(
            P(None, DAP, None),
            P(DAP, "xh", None),
            P(None, "xh"),
            P(),
            P("xh", None),
            P(),
            P(),
            P(),
        ),
        out_specs=P(DAP, "xh", None),
        check_vma=False,
    )
```

```python
import jax
import jax.numpy as jnp
from jax import lax
from jax.experimental import pallas as pl
from jax.experimental.pallas import tpu as pltpu
from jax.sharding import Mesh
from jax.sharding import PartitionSpec as P

DAP = ("yh", "yl", "xl", "z", "core")
PLANE = ("yl", "xl", "core")
CHIP = ("yh", "yl", "xl", "z", "xh")
F32 = jnp.float32
BF16 = jnp.bfloat16
VMEM = pl.BlockSpec(memory_space=pltpu.VMEM)
SMEM = pl.BlockSpec(memory_space=pltpu.SMEM)


def dot(a, b, dims):
    return lax.dot_general(a, b, (dims, ((), ())), preferred_element_type=F32)


def standardized(x, axis):
    mean = jnp.mean(x, axis=axis, keepdims=True)
    centred = x - mean
    var = jnp.mean(centred * centred, axis=axis, keepdims=True)
    return centred * lax.rsqrt(var + 1e-05)


def on_core(kernel, outs, n_in, scratch=(), scalars=0, cost=None, limit=12):
    return pl.pallas_call(
        kernel,
        out_shape=outs,
        in_specs=[SMEM if i < scalars else VMEM for i in range(n_in)],
        out_specs=jax.tree.map(lambda _: VMEM, outs),
        scratch_shapes=scratch,
        compiler_params=pltpu.CompilerParams(vmem_limit_bytes=limit << 20),
        cost_estimate=cost,
    )


def cost(us):
    return pl.CostEstimate(flops=int(us * 1e9), bytes_accessed=int(us * 3e6), transcendentals=0)


def first_kernel(msa_hbm, second_hbm, right_ref, norm_ref, msa_ref, second_ref, sems):
    fetches = [
        pltpu.make_async_copy(msa_hbm, msa_ref, sems.at[0]),
        pltpu.make_async_copy(second_hbm, second_ref, sems.at[1]),
    ]
    for fetch in fetches:
        fetch.start()
    for fetch in fetches:
        fetch.wait()
    for i in range(4):
        normed = standardized(msa_ref[:, i, :].astype(F32), -1).astype(BF16)
        norm_ref[i] = normed
        right = dot(second_ref[...], normed, ((1,), (1,))).astype(BF16)
        for z in range(16):
            right_ref[z, i * 32 : (i + 1) * 32, :] = right


def firsts(msa, second_t):
    return pl.pallas_call(
        first_kernel,
        out_shape=(jax.ShapeDtypeStruct((16, 128, 128), BF16), jax.ShapeDtypeStruct((4, 128, 256), BF16)),
        in_specs=[pl.BlockSpec(memory_space=pl.ANY)] * 2,
        out_specs=(VMEM, VMEM),
        scratch_shapes=[
            pltpu.VMEM((128, 4, 256), BF16),
            pltpu.VMEM((32, 256), BF16),
            pltpu.SemaphoreType.DMA((2,)),
        ],
        compiler_params=pltpu.CompilerParams(vmem_limit_bytes=60 << 20),
        cost_estimate=cost(1),
    )(msa, second_t)


def pack_kernel(me_ref, norm_ref, own_ref, other_ref, couple_ref, *packed_refs):
    me, mex = me_ref[0], me_ref[1]
    for i in range(4):
        normed = norm_ref[i]
        lo = dot(own_ref[...], normed, ((1,), (1,))).astype(BF16)
        hi = dot(other_ref[...], normed, ((1,), (1,))).astype(BF16)
        for m in range(8):
            packed_refs[m][pl.ds(pl.multiple_of(128 + i * 32 + mex * 16, 16), 16), :] = lo
            packed_refs[m][pl.ds(pl.multiple_of(144 + i * 32 - mex * 16, 16), 16), :] = hi
    row = lax.broadcasted_iota(jnp.int32, (8, 128), 0)
    for m in range(8):
        g = m ^ me
        keep = (row < 4) == (g % 2 == 0)
        for i in range(4):
            for zz in range(4):
                start = pl.multiple_of((g // 2) * 64 + zz * 16, 16)
                pair = couple_ref[i, pl.ds(start, 16), :].astype(F32)
                a, b = pair[:8], pair[8:]
                low = jnp.where(keep, a, pltpu.roll(a, 4, 0))
                high = jnp.where(keep, b, pltpu.roll(b, 4, 0))
                rows = slice(i * 32 + zz * 8, i * 32 + zz * 8 + 8)
                packed_refs[m][rows, :] = jnp.where(row < 4, low, high).astype(BF16)


def packs(me, normed, own_t, other_t, couple):
    return on_core(
        pack_kernel, (jax.ShapeDtypeStruct((256, 128), BF16),) * 8, 5, scalars=1, cost=cost(1)
    )(me, normed, own_t, other_t, couple)


def weight_kernel(me_ref, own_ref, other_ref, wide_ref, w_scr):
    mex = me_ref[1]
    w_scr[pl.ds(pl.multiple_of(mex * 512, 512), 512), :] = own_ref[...].astype(F32)
    w_scr[pl.ds(pl.multiple_of(512 - mex * 512, 512), 512), :] = other_ref[...].astype(F32)
    blank = jnp.zeros((32, 128), BF16)
    for e in range(32):
        w = w_scr[pl.ds(e, 32, stride=32), :].astype(BF16)
        wide_ref[e * 64 : e * 64 + 32, 0:128] = w
        wide_ref[e * 64 : e * 64 + 32, 128:256] = blank
        wide_ref[e * 64 + 32 : e * 64 + 64, 0:128] = blank
        wide_ref[e * 64 + 32 : e * 64 + 64, 128:256] = w


def weights(me, own, other):
    return on_core(
        weight_kernel,
        jax.ShapeDtypeStruct((2048, 256), BF16),
        3,
        [pltpu.VMEM((1024, 128), F32)],
        scalars=1,
        cost=cost(1),
    )(me, own, other)


def pair_kernel(me_ref, right_ref, *rest):
    packed_refs, wide_ref, entry_ref = rest[:8], rest[8], rest[9]
    lifted_refs, cols_ref = rest[10:18], rest[18]
    rows_scr, lhs_scr, cols_scr = rest[19:]
    me = me_ref[0]
    for z in range(8):
        for j in range(4):
            rows_scr[pl.ds(z * 4 + j, 32, stride=32), :] = right_ref[
                me_ref[1] * 8 + z, j * 32 : (j + 1) * 32, :
            ].astype(F32)
    lefts = jnp.concatenate([packed_refs[m][128:256, :] for m in range(8)], axis=0)
    low = lax.broadcasted_iota(jnp.int32, (32, 128), 1) < 64
    for part in range(4):
        rows = rows_scr[part * 256 : (part + 1) * 256, :].astype(BF16)
        outer = dot(rows, lefts, ((1,), (1,)))
        for e in range(4):
            for m in range(8):
                lanes = slice(m * 128, (m + 1) * 128)
                a = outer[e * 64 : e * 64 + 32, lanes]
                b = outer[e * 64 + 32 : e * 64 + 64, lanes]
                rows = slice(m * 32, (m + 1) * 32)
                at = slice((part * 4 + e) * 128, (part * 4 + e + 1) * 128)
                lhs_scr[0, rows, at] = jnp.where(low, a, pltpu.roll(b, 64, 1)).astype(BF16)
                lhs_scr[1, rows, at] = jnp.where(low, pltpu.roll(a, 64, 1), b).astype(BF16)
    for half in range(2):
        update = [
            dot(lhs_scr[p, half * 128 : (half + 1) * 128, :], wide_ref[...], ((1,), (0,))) for p in range(2)
        ]
        for mm in range(4):
            m = half * 4 + mm
            normed = []
            for i in range(4):
                rows = slice(i * 32, (i + 1) * 32)
                lifted = (
                    packed_refs[m][rows, :].astype(F32)
                    + update[i // 2][mm * 32 : (mm + 1) * 32, (i % 2) * 128 : (i % 2 + 1) * 128] * (1.0 / 128)
                ).astype(BF16)
                lifted_refs[m][rows, :] = lifted
                normed.append(standardized(lifted.astype(F32), -1).astype(BF16))
            normed = jnp.concatenate(normed, axis=0)
            p = [dot(entry_ref[q], normed, ((1,), (1,))) for q in range(4)]
            cols_scr[pl.ds(m ^ me, 128, stride=16), :] = jax.nn.sigmoid(p[0]) * p[1]
            cols_scr[pl.ds(8 + (m ^ me), 128, stride=16), :] = jax.nn.sigmoid(p[2]) * p[3]
    for part in range(8):
        cols_ref[part * 16 : (part + 1) * 16] = (
            cols_scr[part * 256 : (part + 1) * 256, :].reshape(16, 16, 128).astype(BF16)
        )


def pairs(me, right, packed, by_e, entry_t):
    out = on_core(
        pair_kernel,
        (jax.ShapeDtypeStruct((128, 128), BF16),) * 8 + (jax.ShapeDtypeStruct((128, 16, 128), BF16),),
        12,
        [
            pltpu.VMEM((1024, 128), F32),
            pltpu.VMEM((2, 256, 2048), BF16),
            pltpu.VMEM((2048, 128), F32),
        ],
        scalars=1,
        limit=14,
        cost=cost(5),
    )(me, right, *packed, by_e, entry_t)
    return out[:8], out[8]


def regrouped(v, lane):
    low, even = lane < 64, (lane // 32) % 2 == 0
    t0 = jnp.where(low, v[0], pltpu.roll(v[2], 64, 1))
    t2 = jnp.where(low, pltpu.roll(v[0], 64, 1), v[2])
    t1 = jnp.where(low, v[1], pltpu.roll(v[3], 64, 1))
    t3 = jnp.where(low, pltpu.roll(v[1], 64, 1), v[3])
    u0 = jnp.where(even, t0, pltpu.roll(t1, 32, 1))
    u1 = jnp.where(even, pltpu.roll(t0, 96, 1), t1)
    u2 = jnp.where(even, t2, pltpu.roll(t3, 32, 1))
    u3 = jnp.where(even, pltpu.roll(t2, 96, 1), t3)
    return u0, u1, u2, u3


def product_kernel(me_ref, cols_ref, mine_ref, theirs_ref, ops_scr, out_scr):
    core = me_ref[2]
    lane = lax.broadcasted_iota(jnp.int32, (8, 128), 1)
    for yh in range(2):
        for z in range(8):
            for part in range(2):
                pieces = []
                for xh in range(2):
                    for x in range(2):
                        src = (((yh * 2 + part) * 2 + x) * 8 + z) * 2 + xh
                        pieces.append(cols_ref[src].astype(F32))
                left = regrouped([p[0:8] for p in pieces], lane)
                right = regrouped([p[8:16] for p in pieces], lane)
                lanes = slice(part * 128, (part + 1) * 128)
                for q in range(4):
                    row = (q * 16 + yh * 8 + z) * 8
                    ops_scr[0, row : row + 8, lanes] = left[q]
                    row = (yh * 32 + q * 8 + z) * 8
                    ops_scr[1, row : row + 8, lanes] = right[q]
    rights = ops_scr[1].astype(BF16)
    for q in range(4):
        prod = dot(ops_scr[0, q * 128 : (q + 1) * 128, :].astype(BF16), rights, ((1,), (1,)))
        for yh in range(2):
            for z in range(8):
                for t in range(4):
                    start = yh * 1024 + (z * 2 + t // 2) * 8 + q * 2 + t % 2
                    out_scr[pl.ds(start, 8, stride=128), :] = prod[
                        (yh * 8 + z) * 8 : (yh * 8 + z + 1) * 8, t * 128 : (t + 1) * 128
                    ]
    for y in range(8):
        rows = slice(y * 16, (y + 1) * 16)
        mine_ref[rows] = out_scr[pl.ds(pl.multiple_of((y * 2 + core) * 128, 128), 128), :].reshape(16, 8, 128)
        theirs_ref[rows] = (
            out_scr[pl.ds(pl.multiple_of((y * 2 + 1 - core) * 128, 128), 128), :].reshape(16, 8, 128).astype(BF16)
        )


def products(me, cols):
    return on_core(
        product_kernel,
        (jax.ShapeDtypeStruct((128, 8, 128), F32), jax.ShapeDtypeStruct((128, 8, 128), BF16)),
        2,
        [pltpu.VMEM((2, 512, 256), F32), pltpu.VMEM((2048, 128), F32)],
        scalars=1,
        cost=cost(3),
    )(me, cols)


def crossed(scr, out_row):
    row = lax.broadcasted_iota(jnp.int32, (8, 128), 0)
    res = []
    for m in range(4):
        a, b = scr[out_row + m * 8 : out_row + m * 8 + 8, :], scr[out_row + 32 + m * 8 : out_row + 40 + m * 8, :]
        res.append(jnp.where(row < 4, a, pltpu.roll(b, 4, 0)))
        res.append(jnp.where(row < 4, pltpu.roll(a, 4, 0), b))
    return jnp.concatenate(res, axis=0)


def gate_kernel(me_ref, *rest):
    own_refs, w_ref, gate_ref, base_ref, gate_scr, base_scr = rest[:8], *rest[8:]
    me = me_ref[0]
    for m in range(8):
        x = own_refs[m][...].astype(F32)
        normed = standardized(x, -1).astype(BF16)
        gate = jax.nn.sigmoid(dot(normed, w_ref[...], ((1,), (0,))))
        for i in range(4):
            rows = pl.ds(pl.multiple_of(i * 256 + (m ^ me) * 32, 32), 32)
            gate_scr[rows, :] = gate[i * 32 : (i + 1) * 32]
            base_scr[rows, :] = x[i * 32 : (i + 1) * 32]
    for b in range(16):
        gate_ref[b * 64 : (b + 1) * 64, :] = crossed(gate_scr, b * 64)
        base_ref[b * 64 : (b + 1) * 64, :] = crossed(base_scr, b * 64)


def gates(me, own, w):
    return on_core(
        gate_kernel,
        (jax.ShapeDtypeStruct((1024, 128), F32), jax.ShapeDtypeStruct((1024, 128), F32)),
        10,
        [pltpu.VMEM((1024, 128), F32), pltpu.VMEM((1024, 128), F32)],
        scalars=1,
        cost=cost(2),
    )(me, *own, w)


def final_kernel(mixed_ref, gate_ref, base_ref, w_ref, out_ref, norm_scr, mm_scr):
    tri_n = standardized(mixed_ref[...].astype(F32), 0)
    norm_scr[...] = tri_n.reshape(1024, 128)
    for i in range(4):
        for t in range(2):
            x = norm_scr[pl.ds(i * 2 + t, 128, stride=8), :].astype(BF16)
            out = dot(x, w_ref[...], ((0,), (0,)))
            for j in range(2):
                for z in range(8):
                    row = (j * 8 + z) * 8
                    mm_scr[pl.ds(i * 256 + z * 4 + t * 2 + j, 8, stride=32), :] = out[row : row + 8]
    for b in range(16):
        rows = slice(b * 64, (b + 1) * 64)
        out_ref[rows, :] = (base_ref[rows, :] + gate_ref[rows, :] * crossed(mm_scr, b * 64)).astype(BF16)


def finals(mixed, gate, base, w):
    return on_core(
        final_kernel,
        jax.ShapeDtypeStruct((1024, 128), BF16),
        4,
        [pltpu.VMEM((1024, 128), F32), pltpu.VMEM((1024, 128), F32)],
        cost=cost(2),
    )(mixed, gate, base, w)


def exchanged(x, axes):
    return lax.all_to_all(x, axes, split_axis=0, concat_axis=0, tiled=True)


def partner(x, axis):
    return lax.ppermute(x, axis, [(0, 1), (1, 0)])


def to_peers(pieces):
    sent = [lax.ppermute(pieces[m], PLANE, [(i, i ^ m) for i in range(8)]) for m in range(1, 8)]
    return [pieces[0], *sent]


def per_device(msa, couple, first, second, w_out, entry, w_gate, w_final):
    at = {name: lax.axis_index(name) for name in ("yh", "yl", "xl", "core", "xh")}
    me = jnp.stack(
        [at["yl"] * 4 + at["xl"] * 2 + at["core"], at["xh"], at["core"], (at["yh"] == at["xh"]).astype(jnp.int32)]
    ).astype(jnp.int32)
    right, normed = firsts(msa, second.T)
    first_t, w_out, right, normed = lax.optimization_barrier((first.T, w_out, right, normed))
    right = exchanged(right, ("yh", "z"))
    first_other = partner(first_t, "xh")
    w_other = partner(w_out, "xh")
    packed = to_peers(packs(me, normed, first_t, first_other, couple))
    by_e = weights(me, w_out, w_other)
    lifted, cols = pairs(me, right, packed, by_e, jnp.swapaxes(entry, 1, 2))
    cols = exchanged(cols, CHIP)
    gate, base = gates(me, to_peers(lifted), w_gate)
    me, gate, base = lax.optimization_barrier((me, gate, base))
    mine, theirs = products(me, cols)
    summed = (mine + partner(theirs, "core").astype(F32)).astype(BF16)
    mixed = exchanged(summed, CHIP)
    return finals(mixed, gate, base, w_final).reshape(4, 256, 128)


def solution(mesh):
    torus = Mesh(mesh.devices.reshape(2, 2, 2, 8, 2, 2), ("yh", "yl", "xl", "z", "core", "xh"))
    return jax.shard_map(
        per_device,
        mesh=torus,
        in_specs=(
            P(None, DAP, None),
            P(DAP, "xh", None),
            P(None, "xh"),
            P(),
            P("xh", None),
            P(),
            P(),
            P(),
        ),
        out_specs=P(DAP, "xh", None),
        check_vma=False,
    )
```

```python
import jax
import jax.numpy as jnp
from jax import lax
from jax.experimental import pallas as pl
from jax.experimental.pallas import tpu as pltpu
from jax.sharding import Mesh
from jax.sharding import PartitionSpec as P

DAP = ("yh", "yl", "xl", "z", "core")
PLANE = ("yl", "xl", "core")
CHIP = ("yh", "yl", "xl", "z", "xh")
F32 = jnp.float32
BF16 = jnp.bfloat16
VMEM = pl.BlockSpec(memory_space=pltpu.VMEM)
SMEM = pl.BlockSpec(memory_space=pltpu.SMEM)


def dot(a, b, dims):
    return lax.dot_general(a, b, (dims, ((), ())), preferred_element_type=F32)


def standardized(x, axis):
    mean = jnp.mean(x, axis=axis, keepdims=True)
    centred = x - mean
    var = jnp.mean(centred * centred, axis=axis, keepdims=True)
    return centred * lax.rsqrt(var + 1e-05)


def on_core(kernel, outs, n_in, scratch=(), scalars=0, cost=None, limit=12):
    return pl.pallas_call(
        kernel,
        out_shape=outs,
        in_specs=[SMEM if i < scalars else VMEM for i in range(n_in)],
        out_specs=jax.tree.map(lambda _: VMEM, outs),
        scratch_shapes=scratch,
        compiler_params=pltpu.CompilerParams(vmem_limit_bytes=limit << 20),
        cost_estimate=cost,
    )


def cost(us):
    return pl.CostEstimate(flops=int(us * 1e9), bytes_accessed=int(us * 3e6), transcendentals=0)


def first_kernel(msa_hbm, second_hbm, right_ref, norm_ref, msa_ref, second_ref, sems):
    fetches = [
        pltpu.make_async_copy(msa_hbm, msa_ref, sems.at[0]),
        pltpu.make_async_copy(second_hbm, second_ref, sems.at[1]),
    ]
    for fetch in fetches:
        fetch.start()
    for fetch in fetches:
        fetch.wait()
    for i in range(4):
        normed = standardized(msa_ref[:, i, :].astype(F32), -1).astype(BF16)
        norm_ref[i] = normed
        right = dot(second_ref[...], normed, ((1,), (1,))).astype(BF16)
        for z in range(16):
            right_ref[z, i * 32 : (i + 1) * 32, :] = right


def firsts(msa, second_t):
    return pl.pallas_call(
        first_kernel,
        out_shape=(jax.ShapeDtypeStruct((16, 128, 128), BF16), jax.ShapeDtypeStruct((4, 128, 256), BF16)),
        in_specs=[pl.BlockSpec(memory_space=pl.ANY)] * 2,
        out_specs=(VMEM, VMEM),
        scratch_shapes=[
            pltpu.VMEM((128, 4, 256), BF16),
            pltpu.VMEM((32, 256), BF16),
            pltpu.SemaphoreType.DMA((2,)),
        ],
        compiler_params=pltpu.CompilerParams(vmem_limit_bytes=60 << 20),
        cost_estimate=cost(1),
    )(msa, second_t)


def pack_kernel(me_ref, norm_ref, own_ref, other_ref, couple_ref, *packed_refs):
    me, mex = me_ref[0], me_ref[1]
    for i in range(4):
        normed = norm_ref[i]
        lo = dot(own_ref[...], normed, ((1,), (1,))).astype(BF16)
        hi = dot(other_ref[...], normed, ((1,), (1,))).astype(BF16)
        for m in range(8):
            packed_refs[m][pl.ds(pl.multiple_of(128 + i * 32 + mex * 16, 16), 16), :] = lo
            packed_refs[m][pl.ds(pl.multiple_of(144 + i * 32 - mex * 16, 16), 16), :] = hi
    row = lax.broadcasted_iota(jnp.int32, (8, 128), 0)
    for m in range(8):
        g = m ^ me
        keep = (row < 4) == (g % 2 == 0)
        for i in range(4):
            for zz in range(4):
                start = pl.multiple_of((g // 2) * 64 + zz * 16, 16)
                pair = couple_ref[i, pl.ds(start, 16), :].astype(F32)
                a, b = pair[:8], pair[8:]
                low = jnp.where(keep, a, pltpu.roll(a, 4, 0))
                high = jnp.where(keep, b, pltpu.roll(b, 4, 0))
                rows = slice(i * 32 + zz * 8, i * 32 + zz * 8 + 8)
                packed_refs[m][rows, :] = jnp.where(row < 4, low, high).astype(BF16)


def packs(me, normed, own_t, other_t, couple):
    return on_core(
        pack_kernel, (jax.ShapeDtypeStruct((256, 128), BF16),) * 8, 5, scalars=1, cost=cost(5)
    )(me, normed, own_t, other_t, couple)


def weight_kernel(me_ref, own_ref, other_ref, wide_ref, w_scr):
    mex = me_ref[1]
    w_scr[pl.ds(pl.multiple_of(mex * 512, 512), 512), :] = own_ref[...].astype(F32)
    w_scr[pl.ds(pl.multiple_of(512 - mex * 512, 512), 512), :] = other_ref[...].astype(F32)
    blank = jnp.zeros((32, 128), BF16)
    for e in range(32):
        w = w_scr[pl.ds(e, 32, stride=32), :].astype(BF16)
        wide_ref[e * 64 : e * 64 + 32, 0:128] = w
        wide_ref[e * 64 : e * 64 + 32, 128:256] = blank
        wide_ref[e * 64 + 32 : e * 64 + 64, 0:128] = blank
        wide_ref[e * 64 + 32 : e * 64 + 64, 128:256] = w


def weights(me, own, other):
    return on_core(
        weight_kernel,
        jax.ShapeDtypeStruct((2048, 256), BF16),
        3,
        [pltpu.VMEM((1024, 128), F32)],
        scalars=1,
        cost=cost(5),
    )(me, own, other)


def pair_kernel(me_ref, right_ref, *rest):
    packed_refs, wide_ref, entry_ref = rest[:8], rest[8], rest[9]
    lifted_refs, cols_ref = rest[10:18], rest[18]
    rows_scr, lhs_scr, cols_scr = rest[19:]
    me = me_ref[0]
    for z in range(8):
        for j in range(4):
            rows_scr[pl.ds(z * 4 + j, 32, stride=32), :] = right_ref[
                me_ref[1] * 8 + z, j * 32 : (j + 1) * 32, :
            ].astype(F32)
    lefts = jnp.concatenate([packed_refs[m][128:256, :] for m in range(8)], axis=0)
    low = lax.broadcasted_iota(jnp.int32, (32, 128), 1) < 64
    for part in range(4):
        rows = rows_scr[part * 256 : (part + 1) * 256, :].astype(BF16)
        outer = dot(rows, lefts, ((1,), (1,)))
        for e in range(4):
            for m in range(8):
                lanes = slice(m * 128, (m + 1) * 128)
                a = outer[e * 64 : e * 64 + 32, lanes]
                b = outer[e * 64 + 32 : e * 64 + 64, lanes]
                rows = slice(m * 32, (m + 1) * 32)
                at = slice((part * 4 + e) * 128, (part * 4 + e + 1) * 128)
                lhs_scr[0, rows, at] = jnp.where(low, a, pltpu.roll(b, 64, 1)).astype(BF16)
                lhs_scr[1, rows, at] = jnp.where(low, pltpu.roll(a, 64, 1), b).astype(BF16)
    for half in range(2):
        update = [
            dot(lhs_scr[p, half * 128 : (half + 1) * 128, :], wide_ref[...], ((1,), (0,))) for p in range(2)
        ]
        for mm in range(4):
            m = half * 4 + mm
            normed = []
            for i in range(4):
                rows = slice(i * 32, (i + 1) * 32)
                lifted = (
                    packed_refs[m][rows, :].astype(F32)
                    + update[i // 2][mm * 32 : (mm + 1) * 32, (i % 2) * 128 : (i % 2 + 1) * 128] * (1.0 / 128)
                ).astype(BF16)
                lifted_refs[m][rows, :] = lifted
                normed.append(standardized(lifted.astype(F32), -1).astype(BF16))
            normed = jnp.concatenate(normed, axis=0)
            p = [dot(entry_ref[q], normed, ((1,), (1,))) for q in range(4)]
            cols_scr[pl.ds(m ^ me, 128, stride=16), :] = jax.nn.sigmoid(p[0]) * p[1]
            cols_scr[pl.ds(8 + (m ^ me), 128, stride=16), :] = jax.nn.sigmoid(p[2]) * p[3]
    for part in range(8):
        cols_ref[part * 16 : (part + 1) * 16] = (
            cols_scr[part * 256 : (part + 1) * 256, :].reshape(16, 16, 128).astype(BF16)
        )


def pairs(me, right, packed, by_e, entry_t):
    out = on_core(
        pair_kernel,
        (jax.ShapeDtypeStruct((128, 128), BF16),) * 8 + (jax.ShapeDtypeStruct((128, 16, 128), BF16),),
        12,
        [
            pltpu.VMEM((1024, 128), F32),
            pltpu.VMEM((2, 256, 2048), BF16),
            pltpu.VMEM((2048, 128), F32),
        ],
        scalars=1,
        limit=14,
        cost=cost(5),
    )(me, right, *packed, by_e, entry_t)
    return out[:8], out[8]


def regrouped(v, lane):
    low, even = lane < 64, (lane // 32) % 2 == 0
    t0 = jnp.where(low, v[0], pltpu.roll(v[2], 64, 1))
    t2 = jnp.where(low, pltpu.roll(v[0], 64, 1), v[2])
    t1 = jnp.where(low, v[1], pltpu.roll(v[3], 64, 1))
    t3 = jnp.where(low, pltpu.roll(v[1], 64, 1), v[3])
    u0 = jnp.where(even, t0, pltpu.roll(t1, 32, 1))
    u1 = jnp.where(even, pltpu.roll(t0, 96, 1), t1)
    u2 = jnp.where(even, t2, pltpu.roll(t3, 32, 1))
    u3 = jnp.where(even, pltpu.roll(t2, 96, 1), t3)
    return u0, u1, u2, u3


def product_kernel(me_ref, cols_ref, mine_ref, theirs_ref, ops_scr, out_scr):
    core = me_ref[2]
    lane = lax.broadcasted_iota(jnp.int32, (8, 128), 1)
    for yh in range(2):
        for z in range(8):
            for part in range(2):
                pieces = []
                for xh in range(2):
                    for x in range(2):
                        src = (((yh * 2 + part) * 2 + x) * 8 + z) * 2 + xh
                        pieces.append(cols_ref[src].astype(F32))
                left = regrouped([p[0:8] for p in pieces], lane)
                right = regrouped([p[8:16] for p in pieces], lane)
                lanes = slice(part * 128, (part + 1) * 128)
                for q in range(4):
                    row = (q * 16 + yh * 8 + z) * 8
                    ops_scr[0, row : row + 8, lanes] = left[q]
                    row = (yh * 32 + q * 8 + z) * 8
                    ops_scr[1, row : row + 8, lanes] = right[q]
    rights = ops_scr[1].astype(BF16)
    for q in range(4):
        prod = dot(ops_scr[0, q * 128 : (q + 1) * 128, :].astype(BF16), rights, ((1,), (1,)))
        for yh in range(2):
            for z in range(8):
                for t in range(4):
                    start = yh * 1024 + (z * 2 + t // 2) * 8 + q * 2 + t % 2
                    out_scr[pl.ds(start, 8, stride=128), :] = prod[
                        (yh * 8 + z) * 8 : (yh * 8 + z + 1) * 8, t * 128 : (t + 1) * 128
                    ]
    for y in range(8):
        rows = slice(y * 16, (y + 1) * 16)
        mine_ref[rows] = out_scr[pl.ds(pl.multiple_of((y * 2 + core) * 128, 128), 128), :].reshape(16, 8, 128)
        theirs_ref[rows] = (
            out_scr[pl.ds(pl.multiple_of((y * 2 + 1 - core) * 128, 128), 128), :].reshape(16, 8, 128).astype(BF16)
        )


def products(me, cols):
    return on_core(
        product_kernel,
        (jax.ShapeDtypeStruct((128, 8, 128), F32), jax.ShapeDtypeStruct((128, 8, 128), BF16)),
        2,
        [pltpu.VMEM((2, 512, 256), F32), pltpu.VMEM((2048, 128), F32)],
        scalars=1,
        cost=cost(3),
    )(me, cols)


def crossed(scr, out_row):
    row = lax.broadcasted_iota(jnp.int32, (8, 128), 0)
    res = []
    for m in range(4):
        a, b = scr[out_row + m * 8 : out_row + m * 8 + 8, :], scr[out_row + 32 + m * 8 : out_row + 40 + m * 8, :]
        res.append(jnp.where(row < 4, a, pltpu.roll(b, 4, 0)))
        res.append(jnp.where(row < 4, pltpu.roll(a, 4, 0), b))
    return jnp.concatenate(res, axis=0)


def gate_kernel(me_ref, *rest):
    own_refs, w_ref, gate_ref, base_ref, gate_scr, base_scr = rest[:8], *rest[8:]
    me = me_ref[0]
    for m in range(8):
        x = own_refs[m][...].astype(F32)
        normed = standardized(x, -1).astype(BF16)
        gate = jax.nn.sigmoid(dot(normed, w_ref[...], ((1,), (0,))))
        for i in range(4):
            rows = pl.ds(pl.multiple_of(i * 256 + (m ^ me) * 32, 32), 32)
            gate_scr[rows, :] = gate[i * 32 : (i + 1) * 32]
            base_scr[rows, :] = x[i * 32 : (i + 1) * 32]
    for b in range(16):
        gate_ref[b * 64 : (b + 1) * 64, :] = crossed(gate_scr, b * 64)
        base_ref[b * 64 : (b + 1) * 64, :] = crossed(base_scr, b * 64)


def gates(me, own, w):
    return on_core(
        gate_kernel,
        (jax.ShapeDtypeStruct((1024, 128), F32), jax.ShapeDtypeStruct((1024, 128), F32)),
        10,
        [pltpu.VMEM((1024, 128), F32), pltpu.VMEM((1024, 128), F32)],
        scalars=1,
        cost=cost(2),
    )(me, *own, w)


def final_kernel(mixed_ref, gate_ref, base_ref, w_ref, out_ref, norm_scr, mm_scr):
    tri_n = standardized(mixed_ref[...].astype(F32), 0)
    norm_scr[...] = tri_n.reshape(1024, 128)
    for i in range(4):
        for t in range(2):
            x = norm_scr[pl.ds(i * 2 + t, 128, stride=8), :].astype(BF16)
            out = dot(x, w_ref[...], ((0,), (0,)))
            for j in range(2):
                for z in range(8):
                    row = (j * 8 + z) * 8
                    mm_scr[pl.ds(i * 256 + z * 4 + t * 2 + j, 8, stride=32), :] = out[row : row + 8]
    for b in range(16):
        rows = slice(b * 64, (b + 1) * 64)
        out_ref[rows, :] = (base_ref[rows, :] + gate_ref[rows, :] * crossed(mm_scr, b * 64)).astype(BF16)


def finals(mixed, gate, base, w):
    return on_core(
        final_kernel,
        jax.ShapeDtypeStruct((1024, 128), BF16),
        4,
        [pltpu.VMEM((1024, 128), F32), pltpu.VMEM((1024, 128), F32)],
        cost=cost(2),
    )(mixed, gate, base, w)


def exchanged(x, axes):
    return lax.all_to_all(x, axes, split_axis=0, concat_axis=0, tiled=True)


def partner(x, axis):
    return lax.ppermute(x, axis, [(0, 1), (1, 0)])


def to_peers(pieces):
    sent = {m: lax.ppermute(pieces[m], PLANE, [(i, i ^ m) for i in range(8)]) for m in (7, 6, 5, 3, 4, 2, 1)}
    return [pieces[0], *(sent[m] for m in range(1, 8))]


def per_device(msa, couple, first, second, w_out, entry, w_gate, w_final):
    at = {name: lax.axis_index(name) for name in ("yh", "yl", "xl", "core", "xh")}
    me = jnp.stack(
        [at["yl"] * 4 + at["xl"] * 2 + at["core"], at["xh"], at["core"], (at["yh"] == at["xh"]).astype(jnp.int32)]
    ).astype(jnp.int32)
    right, normed = firsts(msa, second.T)
    first_t = first.T
    w_out, right = lax.optimization_barrier((w_out, right))
    right = exchanged(right, ("yh", "z"))
    first_other = partner(first_t, "xh")
    w_other = partner(w_out, "xh")
    packed = to_peers(packs(me, normed, first_t, first_other, couple))
    by_e = weights(me, w_out, w_other)
    lifted, cols = pairs(me, right, packed, by_e, jnp.swapaxes(entry, 1, 2))
    cols = exchanged(cols, CHIP)
    gate, base = gates(me, to_peers(lifted), w_gate)
    me, gate, base = lax.optimization_barrier((me, gate, base))
    mine, theirs = products(me, cols)
    summed = (mine + partner(theirs, "core").astype(F32)).astype(BF16)
    mixed = exchanged(summed, CHIP)
    return finals(mixed, gate, base, w_final).reshape(4, 256, 128)


def solution(mesh):
    torus = Mesh(mesh.devices.reshape(2, 2, 2, 8, 2, 2), ("yh", "yl", "xl", "z", "core", "xh"))
    return jax.shard_map(
        per_device,
        mesh=torus,
        in_specs=(
            P(None, DAP, None),
            P(DAP, "xh", None),
            P(None, "xh"),
            P(),
            P("xh", None),
            P(),
            P(),
            P(),
        ),
        out_specs=P(DAP, "xh", None),
        check_vma=False,
    )
```

```python
import jax
import jax.numpy as jnp
from jax import lax
from jax.experimental import pallas as pl
from jax.experimental.pallas import tpu as pltpu
from jax.sharding import Mesh
from jax.sharding import PartitionSpec as P

DAP = ("yh", "yl", "xl", "z", "core")
PLANE = ("yl", "xl", "core")
CHIP = ("yh", "yl", "xl", "z", "xh")
F32 = jnp.float32
BF16 = jnp.bfloat16
VMEM = pl.BlockSpec(memory_space=pltpu.VMEM)
SMEM = pl.BlockSpec(memory_space=pltpu.SMEM)


def dot(a, b, dims):
    return lax.dot_general(a, b, (dims, ((), ())), preferred_element_type=F32)


def standardized(x, axis):
    mean = jnp.mean(x, axis=axis, keepdims=True)
    centred = x - mean
    var = jnp.mean(centred * centred, axis=axis, keepdims=True)
    return centred * lax.rsqrt(var + 1e-05)


def on_core(kernel, outs, n_in, scratch=(), scalars=0, cost=None, limit=12):
    return pl.pallas_call(
        kernel,
        out_shape=outs,
        in_specs=[SMEM if i < scalars else VMEM for i in range(n_in)],
        out_specs=jax.tree.map(lambda _: VMEM, outs),
        scratch_shapes=scratch,
        compiler_params=pltpu.CompilerParams(vmem_limit_bytes=limit << 20),
        cost_estimate=cost,
    )


def cost(us):
    return pl.CostEstimate(flops=int(us * 1e9), bytes_accessed=int(us * 3e6), transcendentals=0)


def first_kernel(msa_hbm, second_hbm, right_ref, norm_ref, msa_ref, second_ref, sems):
    fetches = [
        pltpu.make_async_copy(msa_hbm, msa_ref, sems.at[0]),
        pltpu.make_async_copy(second_hbm, second_ref, sems.at[1]),
    ]
    for fetch in fetches:
        fetch.start()
    for fetch in fetches:
        fetch.wait()
    for i in range(4):
        normed = standardized(msa_ref[:, i, :].astype(F32), -1).astype(BF16)
        norm_ref[i] = normed
        right = dot(second_ref[...], normed, ((1,), (1,))).astype(BF16)
        for z in range(16):
            right_ref[z, i * 32 : (i + 1) * 32, :] = right


def firsts(msa, second_t):
    return pl.pallas_call(
        first_kernel,
        out_shape=(jax.ShapeDtypeStruct((16, 128, 128), BF16), jax.ShapeDtypeStruct((4, 128, 256), BF16)),
        in_specs=[pl.BlockSpec(memory_space=pl.ANY)] * 2,
        out_specs=(VMEM, VMEM),
        scratch_shapes=[
            pltpu.VMEM((128, 4, 256), BF16),
            pltpu.VMEM((32, 256), BF16),
            pltpu.SemaphoreType.DMA((2,)),
        ],
        compiler_params=pltpu.CompilerParams(vmem_limit_bytes=60 << 20),
        cost_estimate=cost(1),
    )(msa, second_t)


def pack_kernel(me_ref, norm_ref, own_ref, other_ref, couple_ref, *packed_refs):
    me, mex = me_ref[0], me_ref[1]
    for i in range(4):
        normed = norm_ref[i]
        lo = dot(own_ref[...], normed, ((1,), (1,))).astype(BF16)
        hi = dot(other_ref[...], normed, ((1,), (1,))).astype(BF16)
        for m in range(8):
            packed_refs[m][pl.ds(pl.multiple_of(128 + i * 32 + mex * 16, 16), 16), :] = lo
            packed_refs[m][pl.ds(pl.multiple_of(144 + i * 32 - mex * 16, 16), 16), :] = hi
    row = lax.broadcasted_iota(jnp.int32, (8, 128), 0)
    for m in range(8):
        g = m ^ me
        keep = (row < 4) == (g % 2 == 0)
        for i in range(4):
            for zz in range(4):
                start = pl.multiple_of((g // 2) * 64 + zz * 16, 16)
                pair = couple_ref[i, pl.ds(start, 16), :].astype(F32)
                a, b = pair[:8], pair[8:]
                low = jnp.where(keep, a, pltpu.roll(a, 4, 0))
                high = jnp.where(keep, b, pltpu.roll(b, 4, 0))
                rows = slice(i * 32 + zz * 8, i * 32 + zz * 8 + 8)
                packed_refs[m][rows, :] = jnp.where(row < 4, low, high).astype(BF16)


def packs(me, normed, own_t, other_t, couple):
    return on_core(
        pack_kernel, (jax.ShapeDtypeStruct((256, 128), BF16),) * 8, 5, scalars=1, cost=cost(5)
    )(me, normed, own_t, other_t, couple)


def weight_kernel(me_ref, own_ref, other_ref, wide_ref, w_scr):
    mex = me_ref[1]
    w_scr[pl.ds(pl.multiple_of(mex * 512, 512), 512), :] = own_ref[...].astype(F32)
    w_scr[pl.ds(pl.multiple_of(512 - mex * 512, 512), 512), :] = other_ref[...].astype(F32)
    blank = jnp.zeros((32, 128), BF16)
    for e in range(32):
        w = w_scr[pl.ds(e, 32, stride=32), :].astype(BF16)
        wide_ref[e * 64 : e * 64 + 32, 0:128] = w
        wide_ref[e * 64 : e * 64 + 32, 128:256] = blank
        wide_ref[e * 64 + 32 : e * 64 + 64, 0:128] = blank
        wide_ref[e * 64 + 32 : e * 64 + 64, 128:256] = w


def weights(me, own, other):
    return on_core(
        weight_kernel,
        jax.ShapeDtypeStruct((2048, 256), BF16),
        3,
        [pltpu.VMEM((1024, 128), F32)],
        scalars=1,
        cost=cost(5),
    )(me, own, other)


def pair_kernel(me_ref, right_ref, *rest):
    packed_refs, wide_ref, entry_ref = rest[:8], rest[8], rest[9]
    lifted_refs, cols_ref = rest[10:18], rest[18]
    rows_scr, lhs_scr, cols_scr = rest[19:]
    me = me_ref[0]
    for z in range(8):
        for j in range(4):
            rows_scr[pl.ds(z * 4 + j, 32, stride=32), :] = right_ref[
                me_ref[1] * 8 + z, j * 32 : (j + 1) * 32, :
            ].astype(F32)
    lefts = jnp.concatenate([packed_refs[m][128:256, :] for m in range(8)], axis=0)
    low = lax.broadcasted_iota(jnp.int32, (32, 128), 1) < 64
    for part in range(2):
        rows = rows_scr[part * 512 : (part + 1) * 512, :].astype(BF16)
        outer = dot(rows, lefts, ((1,), (1,)))
        for e in range(8):
            for m in range(8):
                lanes = slice(m * 128, (m + 1) * 128)
                a = outer[e * 64 : e * 64 + 32, lanes]
                b = outer[e * 64 + 32 : e * 64 + 64, lanes]
                rows = slice(m * 32, (m + 1) * 32)
                at = slice((part * 8 + e) * 128, (part * 8 + e + 1) * 128)
                lhs_scr[0, rows, at] = jnp.where(low, a, pltpu.roll(b, 64, 1)).astype(BF16)
                lhs_scr[1, rows, at] = jnp.where(low, pltpu.roll(a, 64, 1), b).astype(BF16)
    for half in range(2):
        update = [
            dot(lhs_scr[p, half * 128 : (half + 1) * 128, :], wide_ref[...], ((1,), (0,))) for p in range(2)
        ]
        for mm in range(4):
            m = half * 4 + mm
            normed = []
            for i in range(4):
                rows = slice(i * 32, (i + 1) * 32)
                lifted = (
                    packed_refs[m][rows, :].astype(F32)
                    + update[i // 2][mm * 32 : (mm + 1) * 32, (i % 2) * 128 : (i % 2 + 1) * 128] * (1.0 / 128)
                ).astype(BF16)
                lifted_refs[m][rows, :] = lifted
                normed.append(standardized(lifted.astype(F32), -1).astype(BF16))
            normed = jnp.concatenate(normed, axis=0)
            p = [dot(entry_ref[q], normed, ((1,), (1,))) for q in range(4)]
            cols_scr[pl.ds(m ^ me, 128, stride=16), :] = jax.nn.sigmoid(p[0]) * p[1]
            cols_scr[pl.ds(8 + (m ^ me), 128, stride=16), :] = jax.nn.sigmoid(p[2]) * p[3]
    for part in range(8):
        cols_ref[part * 16 : (part + 1) * 16] = (
            cols_scr[part * 256 : (part + 1) * 256, :].reshape(16, 16, 128).astype(BF16)
        )


def pairs(me, right, packed, by_e, entry_t):
    out = on_core(
        pair_kernel,
        (jax.ShapeDtypeStruct((128, 128), BF16),) * 8 + (jax.ShapeDtypeStruct((128, 16, 128), BF16),),
        12,
        [
            pltpu.VMEM((1024, 128), F32),
            pltpu.VMEM((2, 256, 2048), BF16),
            pltpu.VMEM((2048, 128), F32),
        ],
        scalars=1,
        limit=14,
        cost=cost(5),
    )(me, right, *packed, by_e, entry_t)
    return out[:8], out[8]


def regrouped(v, lane):
    low, even = lane < 64, (lane // 32) % 2 == 0
    t0 = jnp.where(low, v[0], pltpu.roll(v[2], 64, 1))
    t2 = jnp.where(low, pltpu.roll(v[0], 64, 1), v[2])
    t1 = jnp.where(low, v[1], pltpu.roll(v[3], 64, 1))
    t3 = jnp.where(low, pltpu.roll(v[1], 64, 1), v[3])
    u0 = jnp.where(even, t0, pltpu.roll(t1, 32, 1))
    u1 = jnp.where(even, pltpu.roll(t0, 96, 1), t1)
    u2 = jnp.where(even, t2, pltpu.roll(t3, 32, 1))
    u3 = jnp.where(even, pltpu.roll(t2, 96, 1), t3)
    return u0, u1, u2, u3


def product_kernel(me_ref, cols_ref, mine_ref, theirs_ref, ops_scr, out_scr):
    core = me_ref[2]
    lane = lax.broadcasted_iota(jnp.int32, (8, 128), 1)
    for yh in range(2):
        for z in range(8):
            for part in range(2):
                pieces = []
                for xh in range(2):
                    for x in range(2):
                        src = (((yh * 2 + part) * 2 + x) * 8 + z) * 2 + xh
                        pieces.append(cols_ref[src].astype(F32))
                left = regrouped([p[0:8] for p in pieces], lane)
                right = regrouped([p[8:16] for p in pieces], lane)
                lanes = slice(part * 128, (part + 1) * 128)
                for q in range(4):
                    row = (q * 16 + yh * 8 + z) * 8
                    ops_scr[0, row : row + 8, lanes] = left[q]
                    row = (yh * 32 + q * 8 + z) * 8
                    ops_scr[1, row : row + 8, lanes] = right[q]
    rights = ops_scr[1].astype(BF16)
    for q in range(4):
        prod = dot(ops_scr[0, q * 128 : (q + 1) * 128, :].astype(BF16), rights, ((1,), (1,)))
        for yh in range(2):
            for z in range(8):
                for t in range(4):
                    start = yh * 1024 + (z * 2 + t // 2) * 8 + q * 2 + t % 2
                    out_scr[pl.ds(start, 8, stride=128), :] = prod[
                        (yh * 8 + z) * 8 : (yh * 8 + z + 1) * 8, t * 128 : (t + 1) * 128
                    ]
    for y in range(8):
        rows = slice(y * 16, (y + 1) * 16)
        mine_ref[rows] = out_scr[pl.ds(pl.multiple_of((y * 2 + core) * 128, 128), 128), :].reshape(16, 8, 128)
        theirs_ref[rows] = (
            out_scr[pl.ds(pl.multiple_of((y * 2 + 1 - core) * 128, 128), 128), :].reshape(16, 8, 128).astype(BF16)
        )


def products(me, cols):
    return on_core(
        product_kernel,
        (jax.ShapeDtypeStruct((128, 8, 128), F32), jax.ShapeDtypeStruct((128, 8, 128), BF16)),
        2,
        [pltpu.VMEM((2, 512, 256), F32), pltpu.VMEM((2048, 128), F32)],
        scalars=1,
        cost=cost(3),
    )(me, cols)


def crossed(scr, out_row):
    row = lax.broadcasted_iota(jnp.int32, (8, 128), 0)
    res = []
    for m in range(4):
        a, b = scr[out_row + m * 8 : out_row + m * 8 + 8, :], scr[out_row + 32 + m * 8 : out_row + 40 + m * 8, :]
        res.append(jnp.where(row < 4, a, pltpu.roll(b, 4, 0)))
        res.append(jnp.where(row < 4, pltpu.roll(a, 4, 0), b))
    return jnp.concatenate(res, axis=0)


def gate_kernel(me_ref, *rest):
    own_refs, w_ref, gate_ref, base_ref, gate_scr, base_scr = rest[:8], *rest[8:]
    me = me_ref[0]
    for m in range(8):
        x = own_refs[m][...].astype(F32)
        normed = standardized(x, -1).astype(BF16)
        gate = jax.nn.sigmoid(dot(normed, w_ref[...], ((1,), (0,))))
        for i in range(4):
            rows = pl.ds(pl.multiple_of(i * 256 + (m ^ me) * 32, 32), 32)
            gate_scr[rows, :] = gate[i * 32 : (i + 1) * 32]
            base_scr[rows, :] = x[i * 32 : (i + 1) * 32]
    for b in range(16):
        gate_ref[b * 64 : (b + 1) * 64, :] = crossed(gate_scr, b * 64)
        base_ref[b * 64 : (b + 1) * 64, :] = crossed(base_scr, b * 64)


def gates(me, own, w):
    return on_core(
        gate_kernel,
        (jax.ShapeDtypeStruct((1024, 128), F32), jax.ShapeDtypeStruct((1024, 128), F32)),
        10,
        [pltpu.VMEM((1024, 128), F32), pltpu.VMEM((1024, 128), F32)],
        scalars=1,
        cost=cost(2),
    )(me, *own, w)


def final_kernel(mixed_ref, gate_ref, base_ref, w_ref, out_ref, norm_scr, mm_scr):
    tri_n = standardized(mixed_ref[...].astype(F32), 0)
    norm_scr[...] = tri_n.reshape(1024, 128)
    for i in range(4):
        for t in range(2):
            x = norm_scr[pl.ds(i * 2 + t, 128, stride=8), :].astype(BF16)
            out = dot(x, w_ref[...], ((0,), (0,)))
            for j in range(2):
                for z in range(8):
                    row = (j * 8 + z) * 8
                    mm_scr[pl.ds(i * 256 + z * 4 + t * 2 + j, 8, stride=32), :] = out[row : row + 8]
    for b in range(16):
        rows = slice(b * 64, (b + 1) * 64)
        out_ref[rows, :] = (base_ref[rows, :] + gate_ref[rows, :] * crossed(mm_scr, b * 64)).astype(BF16)


def finals(mixed, gate, base, w):
    return on_core(
        final_kernel,
        jax.ShapeDtypeStruct((1024, 128), BF16),
        4,
        [pltpu.VMEM((1024, 128), F32), pltpu.VMEM((1024, 128), F32)],
        cost=cost(2),
    )(mixed, gate, base, w)


def exchanged(x, axes):
    return lax.all_to_all(x, axes, split_axis=0, concat_axis=0, tiled=True)


def partner(x, axis):
    return lax.ppermute(x, axis, [(0, 1), (1, 0)])


def to_peers(pieces):
    sent = {m: lax.ppermute(pieces[m], PLANE, [(i, i ^ m) for i in range(8)]) for m in (7, 6, 5, 3, 4, 2, 1)}
    return [pieces[0], *(sent[m] for m in range(1, 8))]


def per_device(msa, couple, first, second, w_out, entry, w_gate, w_final):
    at = {name: lax.axis_index(name) for name in ("yh", "yl", "xl", "core", "xh")}
    me = jnp.stack(
        [at["yl"] * 4 + at["xl"] * 2 + at["core"], at["xh"], at["core"], (at["yh"] == at["xh"]).astype(jnp.int32)]
    ).astype(jnp.int32)
    right, normed = firsts(msa, second.T)
    first_t = first.T
    w_out, right = lax.optimization_barrier((w_out, right))
    right = exchanged(right, ("yh", "z"))
    first_other = partner(first_t, "xh")
    w_other = partner(w_out, "xh")
    packed = to_peers(packs(me, normed, first_t, first_other, couple))
    by_e = weights(me, w_out, w_other)
    lifted, cols = pairs(me, right, packed, by_e, jnp.swapaxes(entry, 1, 2))
    cols = exchanged(cols, CHIP)
    gate, base = gates(me, to_peers(lifted), w_gate)
    me, gate, base = lax.optimization_barrier((me, gate, base))
    mine, theirs = products(me, cols)
    summed = (mine + partner(theirs, "core").astype(F32)).astype(BF16)
    mixed = exchanged(summed, CHIP)
    return finals(mixed, gate, base, w_final).reshape(4, 256, 128)


def solution(mesh):
    torus = Mesh(mesh.devices.reshape(2, 2, 2, 8, 2, 2), ("yh", "yl", "xl", "z", "core", "xh"))
    return jax.shard_map(
        per_device,
        mesh=torus,
        in_specs=(
            P(None, DAP, None),
            P(DAP, "xh", None),
            P(None, "xh"),
            P(),
            P("xh", None),
            P(),
            P(),
            P(),
        ),
        out_specs=P(DAP, "xh", None),
        check_vma=False,
    )
```
